512 devices in a mesh: dp: 32 (over z, x_hi), mp: 16 (over x_lo, y, core).
Axes of the slice: x: 4 (x_hi: 2, x_lo: 2; x = x_hi * 2 + x_lo), y: 4, z: 16, core: 2. Of those that a mesh axis runs over, the one named last changes fastest.
Arguments:
- tokens: bfloat16 [32768, 2048], P('dp', 'mp'), may hold values from -6 to 6
- norm_gain: bfloat16 [2048], replicated, may hold values from 0.099609375 to 1.8984375
- wi_gate: bfloat16 [2048, 5120], P(None, 'mp'), may hold values from -0.125 to 0.125
- wi_linear: bfloat16 [2048, 5120], P(None, 'mp'), may hold values from -0.125 to 0.125
- wo_out: bfloat16 [5120, 2048], P('mp'), may hold values from -0.078125 to 0.078125
- task_table: float32 [8, 64], replicated, may hold values from -5 to 5
- layer_table: float32 [24, 64], replicated, may hold values from -5 to 5
- task_ids: int32 [256], P('dp'), may hold values from 0 to 7
- layer_index: int32 [1], replicated, may hold values from 0 to 23
- hyper_in: bfloat16 [128, 1024], P(None, 'mp'), may hold values from -0.5 to 0.5
- gen_down: bfloat16 [1024, 131072], P(None, ('mp', 'dp')), may hold values from -0.0078125 to 0.0078125
- gen_up: bfloat16 [1024, 131072], P(None, ('mp', 'dp')), may hold values from -0.046875 to 0.046875
Outputs:
- mixed: bfloat16 [32768, 2048], P('dp', 'mp')
The draws below stay inside these ranges and needn't reach their ends.
All inputs are finite; a program needn't handle non-finite values.
Results may differ from the reference program's by a relative error of at most 0.019.
Values may be sent and summed in bfloat16 or wider, within the bound.
No kernel may reach another device: no remote copies, remote signals or barrier semaphores. Data moves between devices by JAX's collectives and lax.ppermute only.
A program may use at most 64 MiB of HBM per device.

```python
import jax
import jax.numpy as jnp
from jax import lax

D = 2048
FF = 5120
R = 64
HID = 1024
EMB = 64
TASKS = 8
LAYERS = 24
SEQ = 128
SEQS = 256
TOKENS = 32768
N_MP = 16


def touch_ends(drawn, own_key, smallest, top_value):
    shape = drawn.shape
    place = [jax.random.randint(jax.random.fold_in(own_key, axis), (), 0, shape[axis]) for axis in range(len(shape))]
    drawn = drawn.at[tuple(place)].set(smallest)
    longest = shape.index(max(shape))
    place[longest] = (place[longest] + 1) % shape[longest]
    return drawn.at[tuple(place)].set(top_value)


def steps_of(rng, dims, pieces, low, top_value):
    factor_of, own = 1.0, jax.random.fold_in(rng, 6)
    for dim, shards_of in pieces:
        draws = jnp.exp(jax.random.uniform(jax.random.fold_in(own, dim), (shards_of,), jnp.float32, low / len(pieces), top_value / len(pieces)))
        factor_of = factor_of * jnp.repeat(draws, dims[dim] // shards_of).reshape([-1 if axis == dim else 1 for axis in range(len(dims))])
    return factor_of


def noise(stream_key, dims, scale, reach, shards=(), kind=jnp.bfloat16):
    entries = jax.random.normal(stream_key, dims, jnp.float32) * scale
    if len(shards) > 0:
        entries = steps_of(stream_key, dims, shards, -0.22, 0.18) * entries
    return jnp.clip(entries, min=-reach, max=reach).astype(kind)


def setup_inputs(seed: int = 0) -> dict:
    seeds = jax.random.split(jax.random.key(seed), 13)
    tokens = noise(seeds[0], (TOKENS, D), 1.0, 6.0, ((0, 32), (1, 16)))
    norm_gain = jnp.clip(1.0 + 0.18 * jax.random.normal(seeds[1], (D,), jnp.float32), 0.099609375, 1.8984375).astype(jnp.bfloat16)
    wi_gate = noise(seeds[2], (D, FF), D ** -0.5, 0.125, ((1, 16),))
    wi_linear = noise(seeds[3], (D, FF), D ** -0.5, 0.125, ((1, 16),))
    wo_out = noise(seeds[4], (FF, D), FF ** -0.5, 0.078125, ((0, 16),))
    task_table = noise(seeds[5], (TASKS, EMB), 1.0, 5.0, (), jnp.float32)
    layer_table = noise(seeds[6], (LAYERS, EMB), 1.0, 5.0, (), jnp.float32)
    task_ids = touch_ends(jax.random.randint(seeds[7], (SEQS,), 0, TASKS), jax.random.fold_in(seeds[7], 1), 0, TASKS - 1).astype(jnp.int32)
    layer_index = jax.random.randint(seeds[8], (1,), 0, LAYERS).astype(jnp.int32)
    hyper_in = noise(seeds[9], (2 * EMB, HID), (2 * EMB) ** -0.5, 0.5, ((1, 16),))
    gen_down = noise(seeds[10], (HID, D * R), (HID * D // 4) ** -0.5, 0.0078125, ((1, 512),))
    gen_up = noise(seeds[11], (HID, D * R), (HID * R // 4) ** -0.5, 0.046875, ((1, 512),))
    return {"tokens": tokens, "norm_gain": norm_gain, "wi_gate": wi_gate, "wi_linear": wi_linear, "wo_out": wo_out, "task_table": task_table, "layer_table": layer_table, "task_ids": task_ids, "layer_index": layer_index, "hyper_in": hyper_in, "gen_down": gen_down, "gen_up": gen_up}


def reference(tokens, norm_gain, wi_gate, wi_linear, wo_out, task_table, layer_table, task_ids, layer_index, hyper_in, gen_down, gen_up):
    layer_row = jnp.take(layer_table, layer_index, axis=0)
    embed = jnp.concatenate([task_table, jnp.broadcast_to(layer_row, (TASKS, EMB))], axis=1).astype(jnp.bfloat16)
    hidden = jnp.maximum(jnp.dot(embed, hyper_in, preferred_element_type=jnp.float32), 0.0).astype(jnp.bfloat16)
    down_all = jnp.dot(hidden, gen_down, preferred_element_type=jnp.float32).astype(jnp.bfloat16)
    up_all = jnp.dot(hidden, gen_up, preferred_element_type=jnp.float32).astype(jnp.bfloat16)
    wide = tokens.astype(jnp.float32)
    scale = jax.lax.rsqrt(lax.optimization_barrier(jnp.mean(wide * wide, axis=-1, keepdims=True)) + 1e-06)
    normed = (wide * scale * norm_gain.astype(jnp.float32)).astype(jnp.bfloat16)
    gate = jnp.dot(normed, wi_gate, preferred_element_type=jnp.float32)
    linear = jnp.dot(normed, wi_linear, preferred_element_type=jnp.float32)
    act = (jax.nn.gelu(gate, approximate=True) * linear).astype(jnp.bfloat16)
    group = FF // N_MP

    def add_group(total, index):
        start = (index * group).astype(jnp.int32)
        cols = lax.dynamic_slice_in_dim(act, start, group, 1)
        rows = lax.dynamic_slice_in_dim(wo_out, start, group, 0)
        piece = jnp.dot(cols, rows, preferred_element_type=jnp.float32).astype(jnp.bfloat16)
        piece = lax.optimization_barrier(piece)
        return (total + piece.astype(jnp.float32), None)
    summed, unused = lax.scan(add_group, jnp.zeros((TOKENS, D), jnp.float32), jnp.arange(N_MP, dtype=jnp.int32))
    ffout = summed.astype(jnp.bfloat16)
    seq_down = jnp.take(down_all, task_ids, axis=0).reshape(SEQS, D, R).astype(jnp.float32)
    seq_up = jnp.take(up_all, task_ids, axis=0).reshape(SEQS, D, R).astype(jnp.float32)
    blocks = ffout.astype(jnp.float32).reshape(SEQS, SEQ, D)
    squeezed = jnp.maximum(jnp.einsum('std,sdr->str', blocks, seq_down), 0.0).astype(jnp.bfloat16)
    expand = jnp.einsum('str,sdr->std', squeezed.astype(jnp.float32), seq_up).reshape(TOKENS, D)
    return (wide + ffout.astype(jnp.float32) + expand).astype(jnp.bfloat16)
```

```python
import jax
import jax.numpy as jnp
from jax import lax
from jax.experimental import pallas as pl
from jax.experimental.pallas import tpu as pltpu
from jax.sharding import PartitionSpec as P

R = 64
CORES = 2
CHIPS = 8
MP = CORES * CHIPS
DP = 32
VMEM = 56 * 1024 * 1024


def matmul(left, right):
    return jnp.dot(left, right, preferred_element_type=jnp.float32)


def matmul_nt(left, right):
    return lax.dot_general(
        left, right, (((1,), (1,)), ((), ())), preferred_element_type=jnp.float32
    )


def exchange(pieces, axis):
    return lax.all_to_all(pieces, axis, split_axis=0, concat_axis=0, tiled=True)


def doubling_gather(shard, axis, size):
    index = lax.axis_index(axis)
    held = shard
    bit = size // 2
    while bit:
        theirs = lax.ppermute(held, axis, [(i, i ^ bit) for i in range(size)])
        upper = (index & bit) != 0
        held = jnp.stack([jnp.where(upper, theirs, held), jnp.where(upper, held, theirs)])
        bit //= 2
    return held


def ffn_body(x_ref, gain_ref, wi_ref, wo_own_ref, wo_other_ref, out_ref):
    wide = jnp.concatenate([x_ref[i] for i in range(MP)], axis=1).astype(jnp.float32)
    scale = lax.rsqrt(jnp.mean(wide * wide, axis=-1, keepdims=True) + 1e-06)
    normed = (wide * scale * gain_ref[...].astype(jnp.float32)).astype(jnp.bfloat16)
    both = matmul_nt(normed, wi_ref[...])
    hid = both.shape[1] // 2
    act = (jax.nn.gelu(both[:, :hid], approximate=True) * both[:, hid:]).astype(jnp.bfloat16)
    own = hid // 2
    sums = matmul(act[:, :own], wo_own_ref[...]) + matmul(act[:, own:], wo_other_ref[...])
    sums = sums.astype(jnp.bfloat16)
    width = out_ref.shape[2]
    for i in range(MP):
        out_ref[i] = sums[:, i * width : (i + 1) * width]


def ffn(x, gain, wi, wo_own, wo_other):
    tile = 256
    rows, width = x.shape[1:]
    whole = lambda a: pl.BlockSpec(a.shape, lambda i: (0, 0))
    return pl.pallas_call(
        ffn_body,
        out_shape=jax.ShapeDtypeStruct((MP, rows, width), jnp.bfloat16),
        grid=(rows // tile,),
        in_specs=[
            pl.BlockSpec((MP, tile, width), lambda i: (0, i, 0)),
            whole(gain),
            whole(wi),
            whole(wo_own),
            whole(wo_other),
        ],
        out_specs=pl.BlockSpec((MP, tile, width), lambda i: (0, i, 0)),
        compiler_params=pltpu.CompilerParams(vmem_limit_bytes=VMEM),
        name="ffn",
    )(x, gain, wi, wo_own, wo_other)


def squeeze_body(ids_ref, parts_ref, down_ref, ffout_ref, squeezed_ref):
    s = pl.program_id(0)
    total = parts_ref[0, 0].astype(jnp.float32)
    for i in range(1, CHIPS):
        total = total + parts_ref[i, 0].astype(jnp.float32)
    ffout = total.astype(jnp.bfloat16)
    ffout_ref[...] = ffout
    sums = matmul(ffout, down_ref[ids_ref[s]]).astype(jnp.bfloat16)
    quarter = sums.shape[0] // 4
    for i in range(2):
        first = sums[2 * i * quarter : (2 * i + 1) * quarter]
        second = sums[(2 * i + 1) * quarter : (2 * i + 2) * quarter]
        squeezed_ref[i] = jnp.concatenate([first, second], axis=1)


def squeeze(task_ids, parts, down):
    rows, width = parts.shape[1:]
    seqs = task_ids.shape[0]
    seq = CORES * rows // seqs
    half = seqs // CORES
    return pl.pallas_call(
        squeeze_body,
        out_shape=(
            jax.ShapeDtypeStruct((CORES * rows, width), jnp.bfloat16),
            jax.ShapeDtypeStruct((2 * seqs, seq // 4, 2 * R), jnp.bfloat16),
        ),
        grid_spec=pltpu.PrefetchScalarGridSpec(
            num_scalar_prefetch=1,
            grid=(seqs,),
            in_specs=[
                pl.BlockSpec((CHIPS, 1, seq, width), lambda s, ids: (0, s // half, s % half, 0)),
                pl.BlockSpec(down.shape, lambda s, ids: (0, 0, 0)),
            ],
            out_specs=(
                pl.BlockSpec((seq, width), lambda s, ids: (s, 0)),
                pl.BlockSpec((2, seq // 4, 2 * R), lambda s, ids: (s, 0, 0)),
            ),
        ),
        compiler_params=pltpu.CompilerParams(vmem_limit_bytes=VMEM),
        name="squeeze",
    )(task_ids, parts.reshape(CHIPS, CORES, rows, width), down)


def relu_body(parts_ref, out_ref):
    total = parts_ref[0].astype(jnp.float32)
    for i in range(1, MP):
        total = total + parts_ref[i].astype(jnp.float32)
    squeezed = jnp.maximum(total, 0.0).astype(jnp.bfloat16)
    for i in range(MP):
        out_ref[i] = squeezed


def relu_for_everyone(parts):
    return pl.pallas_call(
        relu_body,
        out_shape=jax.ShapeDtypeStruct(parts.shape, parts.dtype),
        name="relu_for_everyone",
    )(parts)


def expand_body(ids_ref, tokens_ref, ffout_ref, squeezed_ref, up_ref, out_ref):
    s = pl.program_id(0)
    both = [squeezed_ref[i] for i in range(2)]
    squeezed = jnp.concatenate([both[i][:, j * R : (j + 1) * R] for i in range(2) for j in range(2)])
    expand = matmul_nt(squeezed, up_ref[ids_ref[s]])
    total = tokens_ref[...].astype(jnp.float32) + ffout_ref[...].astype(jnp.float32) + expand
    out_ref[...] = total.astype(jnp.bfloat16)


def expand(task_ids, tokens, ffout, squeezed, up):
    seqs = task_ids.shape[0]
    rows, width = tokens.shape
    seq = rows // seqs
    row_spec = pl.BlockSpec((seq, width), lambda s, ids: (s, 0))
    return pl.pallas_call(
        expand_body,
        out_shape=jax.ShapeDtypeStruct(tokens.shape, tokens.dtype),
        grid_spec=pltpu.PrefetchScalarGridSpec(
            num_scalar_prefetch=1,
            grid=(seqs,),
            in_specs=[
                row_spec,
                row_spec,
                pl.BlockSpec((2, *squeezed.shape[1:]), lambda s, ids: (s, 0, 0)),
                pl.BlockSpec(up.shape, lambda s, ids: (0, 0, 0)),
            ],
            out_specs=row_spec,
        ),
        compiler_params=pltpu.CompilerParams(vmem_limit_bytes=VMEM),
        name="expand",
    )(task_ids, tokens, ffout, squeezed, up)


def per_device(
    tokens,
    norm_gain,
    wi_gate,
    wi_linear,
    wo_out,
    task_table,
    layer_table,
    task_ids,
    layer_index,
    hyper_in,
    gen_down,
    gen_up,
):
    tok_dev, width = tokens.shape
    features = width * MP
    half = tok_dev // CORES

    sent = jnp.broadcast_to(tokens.reshape(1, CORES, half, width), (CHIPS, CORES, half, width))
    gathered = exchange(sent.reshape(MP, half, width), "mp")

    swap = lambda w: lax.ppermute(w, "mp", [(i, i ^ 1) for i in range(MP)])
    gate, linear = wi_gate.T, wi_linear.T
    gate_other, linear_other, wo_other = swap(gate), swap(linear), swap(wo_out)
    wi = jnp.concatenate([gate, gate_other, linear, linear_other], axis=0)

    task_count = task_table.shape[0]
    layer_row = jnp.take(layer_table, layer_index, axis=0)
    embed = jnp.concatenate(
        [task_table, jnp.broadcast_to(layer_row, (task_count, layer_row.shape[1]))], axis=1
    ).astype(jnp.bfloat16)
    hidden_part = jnp.maximum(matmul(embed, hyper_in), 0.0).astype(jnp.bfloat16)
    hidden = doubling_gather(hidden_part, "mp", MP)
    hidden = jnp.transpose(hidden, (4, 3, 2, 1, 0, 5)).reshape(task_count, -1)
    made = jnp.stack(
        [matmul(hidden, gen_down).astype(jnp.bfloat16), matmul(hidden, gen_up).astype(jnp.bfloat16)]
    )
    all_tasks = doubling_gather(made, "dp", DP)
    all_tasks = jnp.transpose(all_tasks, (5, 6, 4, 3, 2, 1, 0, 7))
    adapters = all_tasks.reshape(2, task_count, width, R)

    partial = ffn(gathered, norm_gain.reshape(1, features), wi, wo_out, wo_other)
    ffout, squeeze_part = squeeze(task_ids, exchange(partial, "mp"), adapters[0])
    squeezed = exchange(relu_for_everyone(exchange(squeeze_part, "mp")), "mp")
    return expand(task_ids, tokens, ffout, squeezed, adapters[1])


def solution(mesh):
    return jax.shard_map(
        per_device,
        mesh=mesh,
        in_specs=(
            P("dp", "mp"),
            P(),
            P(None, "mp"),
            P(None, "mp"),
            P("mp", None),
            P(),
            P(),
            P("dp"),
            P(),
            P(None, "mp"),
            P(None, ("mp", "dp")),
            P(None, ("mp", "dp")),
        ),
        out_specs=P("dp", "mp"),
        check_vma=False,
    )
```

```python
import jax
import jax.numpy as jnp
from jax import lax
from jax.experimental import pallas as pl
from jax.experimental.pallas import tpu as pltpu
from jax.sharding import PartitionSpec as P

R = 64
CORES = 2
CHIPS = 8
MP = CORES * CHIPS
DP = 32
SAME_CORE = [[chip * CORES + core for chip in range(CHIPS)] for core in range(CORES)]
VMEM = 32 * 1024 * 1024
FFN_TILE = 256


def matmul(left, right):
    return jnp.dot(left, right, preferred_element_type=jnp.float32)


def matmul_nt(left, right):
    return lax.dot_general(
        left, right, (((1,), (1,)), ((), ())), preferred_element_type=jnp.float32
    )


def exchange(pieces, axis, groups=None):
    return lax.all_to_all(
        pieces, axis, split_axis=0, concat_axis=0, axis_index_groups=groups, tiled=True
    )


def swap_cores(array):
    return lax.ppermute(array, "mp", [(i, i ^ 1) for i in range(MP)])


def doubling_gather(shard, axis, size):
    index = lax.axis_index(axis)
    held = shard
    bit = size // 2
    while bit:
        theirs = lax.ppermute(held, axis, [(i, i ^ bit) for i in range(size)])
        upper = (index & bit) != 0
        held = jnp.stack([jnp.where(upper, theirs, held), jnp.where(upper, held, theirs)])
        bit //= 2
    return held


def in_vmem(array):
    return pltpu.with_memory_space_constraint(array, pltpu.VMEM)


def in_hbm(array):
    return pltpu.with_memory_space_constraint(array, pltpu.HBM)


def whole(array):
    return pl.BlockSpec(memory_space=pltpu.VMEM)


def call(name, body, outs, arrays, scalars=(), place=in_vmem):
    return pl.pallas_call(
        body,
        out_shape=outs,
        in_specs=[pl.BlockSpec(memory_space=pltpu.SMEM) for _ in scalars] + [whole(a) for a in arrays],
        out_specs=jax.tree.map(lambda a: whole(a), outs),
        compiler_params=pltpu.CompilerParams(vmem_limit_bytes=VMEM),
        name=name,
    )(*scalars, *[place(a) for a in arrays])


def spread_body(tokens_ref, given_ref, out_ref, sems):
    me = lax.axis_index("mp") % CORES
    copies = []
    for i in range(CHIPS):
        first, second = out_ref.at[CORES * i + me], out_ref.at[CORES * i + 1 - me]
        copies.append(pltpu.make_async_copy(tokens_ref.at[me], first, sems.at[CORES * i]))
        copies.append(pltpu.make_async_copy(given_ref, second, sems.at[CORES * i + 1]))
    for copy in copies:
        copy.start()
    for copy in copies:
        copy.wait()


def spread(halves, given):
    return pl.pallas_call(
        spread_body,
        out_shape=pltpu.HBM((MP, *given.shape), given.dtype),
        in_specs=[pl.BlockSpec(memory_space=pltpu.HBM), whole(given)],
        out_specs=pl.BlockSpec(memory_space=pltpu.HBM),
        scratch_shapes=[pltpu.SemaphoreType.DMA((MP,))],
        name="spread",
    )(in_hbm(halves), in_vmem(given))


def ffn_body(
    x_ref,
    gain_ref,
    gate_ref,
    gate_other_ref,
    linear_ref,
    linear_other_ref,
    wo_own_ref,
    wo_other_ref,
    out_ref,
    wi_ref,
    wo_ref,
    sums_ref,
    in_sems,
    out_sems,
):
    rows, width = x_ref.shape[1:]
    hid = wo_ref.shape[0]
    own = hid // 2
    placed = [
        (gate_ref, wi_ref.at[pl.ds(0, own)]),
        (gate_other_ref, wi_ref.at[pl.ds(own, own)]),
        (linear_ref, wi_ref.at[pl.ds(hid, own)]),
        (linear_other_ref, wi_ref.at[pl.ds(hid + own, own)]),
        (wo_own_ref, wo_ref.at[pl.ds(0, own)]),
        (wo_other_ref, wo_ref.at[pl.ds(own, own)]),
    ]
    loads = [pltpu.make_async_copy(a, b, in_sems.at[i]) for i, (a, b) in enumerate(placed)]
    for load in loads:
        load.start()
    gain = gain_ref[...].astype(jnp.float32)
    tiles = [pl.ds(k * FFN_TILE, FFN_TILE) for k in range(rows // FFN_TILE)]
    stores = []
    for k, tile in enumerate(tiles):
        wide = jnp.concatenate([x_ref[i, tile] for i in range(MP)], axis=1).astype(jnp.float32)
        scale = lax.rsqrt(jnp.mean(wide * wide, axis=-1, keepdims=True) + 1e-06)
        normed = (wide * scale * gain).astype(jnp.bfloat16)
        if k == 0:
            for load in loads[:4]:
                load.wait()
        both = matmul_nt(normed, wi_ref[...])
        act = (jax.nn.gelu(both[:, :hid], approximate=True) * both[:, hid:]).astype(jnp.bfloat16)
        if k == 0:
            for load in loads[4:]:
                load.wait()
        sums = matmul(act, wo_ref[...]).astype(jnp.bfloat16)
        for i in range(MP):
            sums_ref[k, i] = sums[:, i * width : (i + 1) * width]
        stores.append(pltpu.make_async_copy(sums_ref.at[k], out_ref.at[:, tile], out_sems.at[k]))
        stores[k].start()
    for store in stores:
        store.wait()


def ffn(x, gain, gates, linears, wos):
    rows, width = x.shape[1:]
    own, features = wos[0].shape
    tiles = rows // FFN_TILE
    weights = (*gates, *linears, *wos)
    hbm = pl.BlockSpec(memory_space=pltpu.HBM)
    return pl.pallas_call(
        ffn_body,
        out_shape=pltpu.HBM(x.shape, x.dtype),
        in_specs=[whole(x), whole(gain)] + [hbm] * len(weights),
        out_specs=hbm,
        scratch_shapes=[
            pltpu.VMEM((4 * own, features), x.dtype),
            pltpu.VMEM((2 * own, features), x.dtype),
            pltpu.VMEM((tiles, MP, FFN_TILE, width), x.dtype),
            pltpu.SemaphoreType.DMA((len(weights),)),
            pltpu.SemaphoreType.DMA((tiles,)),
        ],
        compiler_params=pltpu.CompilerParams(vmem_limit_bytes=VMEM),
        name="ffn",
    )(in_vmem(x), in_vmem(gain), *[in_hbm(w) for w in weights])


def squeeze_body(
    ids_ref,
    parts_ref,
    down_ref,
    other_ref,
    kept_out,
    given_out,
    squeezed_out,
    kept_ref,
    given_ref,
    squeezed_ref,
    sems,
):
    rows = parts_ref.shape[1]
    seqs = ids_ref.shape[0]
    seq = rows * CORES // seqs
    quarter = seq // 4
    me = lax.axis_index("mp") % CORES
    for s in range(rows // seq):
        tile = slice(s * seq, (s + 1) * seq)
        task = ids_ref[me * (rows // seq) + s]
        down, other = down_ref[task], other_ref[task]
        ffout = []
        for core in range(CORES):
            total = parts_ref[core, tile].astype(jnp.float32)
            for i in range(1, CHIPS):
                total = total + parts_ref[CORES * i + core, tile].astype(jnp.float32)
            ffout.append(total)
        kept = jnp.where(me == 0, ffout[0], ffout[1]).astype(jnp.bfloat16)
        given = jnp.where(me == 0, ffout[1], ffout[0]).astype(jnp.bfloat16)
        kept_ref[tile] = kept
        given_ref[tile] = given
        sums = (matmul(kept, down) + matmul(given, other)).astype(jnp.bfloat16)
        for i in range(2):
            first = sums[2 * i * quarter : (2 * i + 1) * quarter]
            second = sums[(2 * i + 1) * quarter : (2 * i + 2) * quarter]
            squeezed_ref[2 * s + i] = jnp.concatenate([first, second], axis=1)
    stores = [
        pltpu.make_async_copy(squeezed_ref, squeezed_out, sems.at[0]),
        pltpu.make_async_copy(given_ref, given_out, sems.at[1]),
        pltpu.make_async_copy(kept_ref, kept_out, sems.at[2]),
    ]
    for store in stores:
        store.start()
    for store in stores:
        store.wait()


def squeeze(task_ids, parts, down, other):
    rows, width = parts.shape[1:]
    share = (CHIPS, rows // CHIPS // 2, 2 * R)
    arrays = (parts, down, other)
    hbm = pl.BlockSpec(memory_space=pltpu.HBM)
    return pl.pallas_call(
        squeeze_body,
        out_shape=(
            pltpu.HBM((rows, width), parts.dtype),
            pltpu.HBM((rows, width), parts.dtype),
            pltpu.HBM(share, parts.dtype),
        ),
        in_specs=[pl.BlockSpec(memory_space=pltpu.SMEM)] + [whole(a) for a in arrays],
        out_specs=(hbm, hbm, hbm),
        scratch_shapes=[
            pltpu.VMEM((rows, width), parts.dtype),
            pltpu.VMEM((rows, width), parts.dtype),
            pltpu.VMEM(share, parts.dtype),
            pltpu.SemaphoreType.DMA((3,)),
        ],
        compiler_params=pltpu.CompilerParams(vmem_limit_bytes=VMEM),
        name="squeeze",
    )(task_ids, *[in_vmem(a) for a in arrays])


def relu_body(parts_ref, out_ref):
    total = parts_ref[0].astype(jnp.float32)
    for i in range(1, CHIPS):
        total = total + parts_ref[i].astype(jnp.float32)
    squeezed = jnp.maximum(total, 0.0).astype(jnp.bfloat16)
    for i in range(MP):
        out_ref[i] = squeezed


def relu_for_everyone(parts):
    return call("relu_for_everyone", relu_body, jax.ShapeDtypeStruct((MP, *parts.shape[1:]), parts.dtype), (parts,))


def expand_body(ids_ref, tokens_ref, mine_ref, theirs_ref, squeezed_ref, up_ref, out_ref):
    seqs = ids_ref.shape[0]
    seq = tokens_ref.shape[0] // seqs
    swapped = lax.axis_index("mp") % CORES
    for core in range(CORES):
        for j in range(seqs // CORES):
            s = core * (seqs // CORES) + j
            tile = slice(s * seq, (s + 1) * seq)
            part = slice(j * seq, (j + 1) * seq)
            both = [squeezed_ref[CORES * (2 * j + i) + core] for i in range(2)]
            squeezed = jnp.concatenate(
                [both[i][:, k * R : (k + 1) * R] for i in range(2) for k in range(2)]
            )
            expand = matmul_nt(squeezed, up_ref[ids_ref[s]])
            ffout = jnp.where(swapped == core, mine_ref[part], theirs_ref[part])
            total = tokens_ref[tile].astype(jnp.float32) + ffout.astype(jnp.float32) + expand
            out_ref[tile] = total.astype(jnp.bfloat16)


def expand(task_ids, tokens, mine, theirs, squeezed, up):
    out = jax.ShapeDtypeStruct(tokens.shape, tokens.dtype)
    return call("expand", expand_body, out, (tokens, mine, theirs, squeezed, up), (task_ids,))


def hidden_body(layer_ref, task_table_ref, layer_table_ref, hyper_in_ref, out_ref):
    task_table = task_table_ref[...]
    row = layer_table_ref[pl.ds(layer_ref[0], 1)]
    embed = jnp.concatenate([task_table, jnp.broadcast_to(row, task_table.shape)], axis=1)
    hidden = jnp.maximum(matmul_nt(embed.astype(jnp.bfloat16), hyper_in_ref[...]), 0.0)
    for i in range(MP):
        out_ref[i] = hidden.astype(jnp.bfloat16)


def per_device(
    tokens,
    norm_gain,
    wi_gate,
    wi_linear,
    wo_out,
    task_table,
    layer_table,
    task_ids,
    layer_index,
    hyper_in,
    gen_down,
    gen_up,
):
    tok_dev, width = tokens.shape
    features = width * MP
    half = tok_dev // CORES
    core = lax.axis_index("mp") % CORES
    task_count = task_table.shape[0]

    halves = tokens.reshape(CORES, half, width)
    given = swap_cores(lax.dynamic_index_in_dim(halves, 1 - core, 0, keepdims=False))

    share = hyper_in.shape[1]
    hidden = call(
        "hidden",
        hidden_body,
        jax.ShapeDtypeStruct((MP, task_count, share), jnp.bfloat16),
        (task_table, layer_table, hyper_in.T),
        (layer_index,),
        in_hbm,
    )
    hidden = exchange(hidden, "mp")

    sent, hidden = lax.optimization_barrier((spread(halves, given), hidden))
    gathered = exchange(sent, "mp", SAME_CORE)

    gate, linear = wi_gate.T, wi_linear.T
    gate_other, linear_other, wo_other = swap_cores(gate), swap_cores(linear), swap_cores(wo_out)

    hidden = jnp.moveaxis(hidden, 0, 1).reshape(task_count, -1)
    made = jnp.stack(
        [matmul(hidden, gen_down).astype(jnp.bfloat16), matmul(hidden, gen_up).astype(jnp.bfloat16)]
    )
    all_tasks = doubling_gather(made, "dp", DP)
    all_tasks = jnp.transpose(all_tasks, (5, 6, 4, 3, 2, 1, 0, 7))
    adapters = all_tasks.reshape(2, task_count, width, R)
    down, up = adapters[0], adapters[1]

    partial = ffn(
        gathered,
        norm_gain.reshape(1, features),
        (gate, gate_other),
        (linear, linear_other),
        (wo_out, wo_other),
    )
    parts = exchange(partial, "mp", SAME_CORE)
    mine, given, squeeze_part = squeeze(task_ids, parts, down, swap_cores(down))
    theirs = swap_cores(given)
    squeezed = exchange(relu_for_everyone(exchange(squeeze_part, "mp", SAME_CORE)), "mp")
    return expand(task_ids, tokens, mine, theirs, squeezed, up)


def solution(mesh):
    return jax.shard_map(
        per_device,
        mesh=mesh,
        in_specs=(
            P("dp", "mp"),
            P(),
            P(None, "mp"),
            P(None, "mp"),
            P("mp", None),
            P(),
            P(),
            P("dp"),
            P(),
            P(None, "mp"),
            P(None, ("mp", "dp")),
            P(None, ("mp", "dp")),
        ),
        out_specs=P("dp", "mp"),
        check_vma=False,
    )
```

```python
import jax
import jax.numpy as jnp
from jax import lax
from jax.experimental import pallas as pl
from jax.experimental.pallas import tpu as pltpu
from jax.sharding import PartitionSpec as P

R = 64
CORES = 2
CHIPS = 8
MP = CORES * CHIPS
DP = 32
SAME_CORE = [[chip * CORES + core for chip in range(CHIPS)] for core in range(CORES)]
VMEM = 32 * 1024 * 1024
FFN_TILE = 256


def matmul(left, right):
    return jnp.dot(left, right, preferred_element_type=jnp.float32)


def matmul_nt(left, right):
    return lax.dot_general(
        left, right, (((1,), (1,)), ((), ())), preferred_element_type=jnp.float32
    )


def exchange(pieces, axis, groups=None):
    return lax.all_to_all(
        pieces, axis, split_axis=0, concat_axis=0, axis_index_groups=groups, tiled=True
    )


def swap_cores(array):
    return lax.ppermute(array, "mp", [(i, i ^ 1) for i in range(MP)])


def doubling_gather(shard, axis, size, later):
    index = lax.axis_index(axis)
    held = shard
    bit = size // 2
    while bit:
        theirs = lax.ppermute(held, axis, [(i, i ^ bit) for i in range(size)])
        if held is shard:
            theirs, later = lax.optimization_barrier((theirs, later))
        upper = (index & bit) != 0
        held = jnp.stack([jnp.where(upper, theirs, held), jnp.where(upper, held, theirs)])
        bit //= 2
    return held, later


def in_vmem(array):
    return pltpu.with_memory_space_constraint(array, pltpu.VMEM)


def in_hbm(array):
    return pltpu.with_memory_space_constraint(array, pltpu.HBM)


def whole(array):
    return pl.BlockSpec(memory_space=pltpu.VMEM)


def call(name, body, outs, arrays, scalars=(), place=in_vmem):
    return pl.pallas_call(
        body,
        out_shape=outs,
        in_specs=[pl.BlockSpec(memory_space=pltpu.SMEM) for _ in scalars] + [whole(a) for a in arrays],
        out_specs=jax.tree.map(lambda a: whole(a), outs),
        compiler_params=pltpu.CompilerParams(vmem_limit_bytes=VMEM),
        name=name,
    )(*scalars, *[place(a) for a in arrays])


def spread_body(tokens_ref, given_ref, out_ref, kept_ref, load_sem, sems):
    me = lax.axis_index("mp") % CORES
    load = pltpu.make_async_copy(tokens_ref.at[me], kept_ref, load_sem)
    load.start()
    copies = []
    for i in range(CHIPS):
        second = out_ref.at[CORES * i + 1 - me]
        copies.append(pltpu.make_async_copy(given_ref, second, sems.at[CHIPS + i]))
        copies[i].start()
    load.wait()
    for i in range(CHIPS):
        first = out_ref.at[CORES * i + me]
        copies.append(pltpu.make_async_copy(kept_ref, first, sems.at[i]))
        copies[CHIPS + i].start()
    for copy in copies:
        copy.wait()


def spread(halves, given):
    return pl.pallas_call(
        spread_body,
        out_shape=pltpu.HBM((MP, *given.shape), given.dtype),
        in_specs=[pl.BlockSpec(memory_space=pltpu.HBM), whole(given)],
        out_specs=pl.BlockSpec(memory_space=pltpu.HBM),
        scratch_shapes=[
            pltpu.VMEM(given.shape, given.dtype),
            pltpu.SemaphoreType.DMA(()),
            pltpu.SemaphoreType.DMA((MP,)),
        ],
        name="spread",
    )(in_hbm(halves), in_vmem(given))


def ffn_body(
    x_ref,
    gain_ref,
    gate_ref,
    gate_other_ref,
    linear_ref,
    linear_other_ref,
    wo_own_ref,
    wo_other_ref,
    out_ref,
    normed_ref,
    wi_ref,
    wo_ref,
    sums_ref,
    in_sems,
    out_sems,
):
    rows, width = x_ref.shape[1:]
    hid = wo_ref.shape[0]
    own = hid // 2
    placed = [
        (gate_ref, wi_ref.at[pl.ds(0, own)]),
        (gate_other_ref, wi_ref.at[pl.ds(own, own)]),
        (linear_ref, wi_ref.at[pl.ds(hid, own)]),
        (linear_other_ref, wi_ref.at[pl.ds(hid + own, own)]),
        (wo_own_ref, wo_ref.at[pl.ds(0, own)]),
        (wo_other_ref, wo_ref.at[pl.ds(own, own)]),
    ]
    loads = [pltpu.make_async_copy(a, b, in_sems.at[i]) for i, (a, b) in enumerate(placed)]
    for load in loads:
        load.start()
    gain = gain_ref[...].astype(jnp.float32)
    tiles = [pl.ds(k * FFN_TILE, FFN_TILE) for k in range(rows // FFN_TILE)]
    for tile in tiles:
        wide = jnp.concatenate([x_ref[i, tile] for i in range(MP)], axis=1).astype(jnp.float32)
        scale = lax.rsqrt(jnp.mean(wide * wide, axis=-1, keepdims=True) + 1e-06)
        normed_ref[tile] = (wide * scale * gain).astype(jnp.bfloat16)
    for load in loads[:4]:
        load.wait()
    stores = []
    for k, tile in enumerate(tiles):
        both = matmul_nt(normed_ref[tile], wi_ref[...])
        act = (jax.nn.gelu(both[:, :hid], approximate=True) * both[:, hid:]).astype(jnp.bfloat16)
        if k == 0:
            for load in loads[4:]:
                load.wait()
        sums = matmul(act, wo_ref[...]).astype(jnp.bfloat16)
        for i in range(MP):
            sums_ref[k, i] = sums[:, i * width : (i + 1) * width]
        stores.append(pltpu.make_async_copy(sums_ref.at[k], out_ref.at[:, tile], out_sems.at[k]))
        stores[k].start()
    for store in stores:
        store.wait()


def ffn(x, gain, gates, linears, wos):
    rows, width = x.shape[1:]
    own, features = wos[0].shape
    tiles = rows // FFN_TILE
    weights = (*gates, *linears, *wos)
    hbm = pl.BlockSpec(memory_space=pltpu.HBM)
    return pl.pallas_call(
        ffn_body,
        out_shape=pltpu.HBM(x.shape, x.dtype),
        in_specs=[whole(x), whole(gain)] + [hbm] * len(weights),
        out_specs=hbm,
        scratch_shapes=[
            pltpu.VMEM((rows, features), x.dtype),
            pltpu.VMEM((4 * own, features), x.dtype),
            pltpu.VMEM((2 * own, features), x.dtype),
            pltpu.VMEM((tiles, MP, FFN_TILE, width), x.dtype),
            pltpu.SemaphoreType.DMA((len(weights),)),
            pltpu.SemaphoreType.DMA((tiles,)),
        ],
        compiler_params=pltpu.CompilerParams(vmem_limit_bytes=VMEM),
        name="ffn",
    )(in_vmem(x), in_vmem(gain), *[in_hbm(w) for w in weights])


def squeeze_body(
    ids_ref,
    parts_ref,
    down_ref,
    other_ref,
    kept_out,
    given_out,
    squeezed_out,
    kept_ref,
    given_ref,
    squeezed_ref,
    sems,
):
    rows = parts_ref.shape[1]
    seqs = ids_ref.shape[0]
    seq = rows * CORES // seqs
    quarter = seq // 4
    me = lax.axis_index("mp") % CORES
    for s in range(rows // seq):
        tile = slice(s * seq, (s + 1) * seq)
        task = ids_ref[me * (rows // seq) + s]
        down, other = down_ref[task], other_ref[task]
        ffout = []
        for core in range(CORES):
            total = parts_ref[core, tile].astype(jnp.float32)
            for i in range(1, CHIPS):
                total = total + parts_ref[CORES * i + core, tile].astype(jnp.float32)
            ffout.append(total)
        kept = jnp.where(me == 0, ffout[0], ffout[1]).astype(jnp.bfloat16)
        given = jnp.where(me == 0, ffout[1], ffout[0]).astype(jnp.bfloat16)
        kept_ref[tile] = kept
        given_ref[tile] = given
        sums = (matmul(kept, down) + matmul(given, other)).astype(jnp.bfloat16)
        for i in range(2):
            first = sums[2 * i * quarter : (2 * i + 1) * quarter]
            second = sums[(2 * i + 1) * quarter : (2 * i + 2) * quarter]
            squeezed_ref[2 * s + i] = jnp.concatenate([first, second], axis=1)
    stores = [
        pltpu.make_async_copy(squeezed_ref, squeezed_out, sems.at[0]),
        pltpu.make_async_copy(given_ref, given_out, sems.at[1]),
        pltpu.make_async_copy(kept_ref, kept_out, sems.at[2]),
    ]
    for store in stores:
        store.start()
    for store in stores:
        store.wait()


def squeeze(task_ids, parts, down, other):
    rows, width = parts.shape[1:]
    share = (CHIPS, rows // CHIPS // 2, 2 * R)
    arrays = (parts, down, other)
    hbm = pl.BlockSpec(memory_space=pltpu.HBM)
    return pl.pallas_call(
        squeeze_body,
        out_shape=(
            pltpu.HBM((rows, width), parts.dtype),
            pltpu.HBM((rows, width), parts.dtype),
            pltpu.HBM(share, parts.dtype),
        ),
        in_specs=[pl.BlockSpec(memory_space=pltpu.SMEM)] + [whole(a) for a in arrays],
        out_specs=(hbm, hbm, hbm),
        scratch_shapes=[
            pltpu.VMEM((rows, width), parts.dtype),
            pltpu.VMEM((rows, width), parts.dtype),
            pltpu.VMEM(share, parts.dtype),
            pltpu.SemaphoreType.DMA((3,)),
        ],
        compiler_params=pltpu.CompilerParams(vmem_limit_bytes=VMEM),
        name="squeeze",
    )(task_ids, *[in_vmem(a) for a in arrays])


def relu_body(parts_ref, out_ref):
    total = parts_ref[0].astype(jnp.float32)
    for i in range(1, CHIPS):
        total = total + parts_ref[i].astype(jnp.float32)
    squeezed = jnp.maximum(total, 0.0).astype(jnp.bfloat16)
    for i in range(MP):
        out_ref[i] = squeezed


def relu_for_everyone(parts):
    return call("relu_for_everyone", relu_body, jax.ShapeDtypeStruct((MP, *parts.shape[1:]), parts.dtype), (parts,))


def expand_body(ids_ref, tokens_ref, mine_ref, theirs_ref, squeezed_ref, up_ref, out_ref):
    seqs = ids_ref.shape[0]
    seq = tokens_ref.shape[0] // seqs
    swapped = lax.axis_index("mp") % CORES
    for core in range(CORES):
        for j in range(seqs // CORES):
            s = core * (seqs // CORES) + j
            tile = slice(s * seq, (s + 1) * seq)
            part = slice(j * seq, (j + 1) * seq)
            both = [squeezed_ref[CORES * (2 * j + i) + core] for i in range(2)]
            squeezed = jnp.concatenate(
                [both[i][:, k * R : (k + 1) * R] for i in range(2) for k in range(2)]
            )
            expand = matmul_nt(squeezed, up_ref[ids_ref[s]])
            ffout = jnp.where(swapped == core, mine_ref[part], theirs_ref[part])
            total = tokens_ref[tile].astype(jnp.float32) + ffout.astype(jnp.float32) + expand
            out_ref[tile] = total.astype(jnp.bfloat16)


def expand(task_ids, tokens, mine, theirs, squeezed, up):
    out = jax.ShapeDtypeStruct(tokens.shape, tokens.dtype)
    return call("expand", expand_body, out, (tokens, mine, theirs, squeezed, up), (task_ids,))


def hidden_body(layer_ref, task_table_ref, layer_table_ref, hyper_in_ref, out_ref):
    task_table = task_table_ref[...]
    row = layer_table_ref[pl.ds(layer_ref[0], 1)]
    embed = jnp.concatenate([task_table, jnp.broadcast_to(row, task_table.shape)], axis=1)
    hidden = jnp.maximum(matmul_nt(embed.astype(jnp.bfloat16), hyper_in_ref[...]), 0.0)
    for i in range(MP):
        out_ref[i] = hidden.astype(jnp.bfloat16)


def per_device(
    tokens,
    norm_gain,
    wi_gate,
    wi_linear,
    wo_out,
    task_table,
    layer_table,
    task_ids,
    layer_index,
    hyper_in,
    gen_down,
    gen_up,
):
    tok_dev, width = tokens.shape
    features = width * MP
    half = tok_dev // CORES
    core = lax.axis_index("mp") % CORES
    task_count = task_table.shape[0]

    halves = tokens.reshape(CORES, half, width)
    given = swap_cores(lax.dynamic_index_in_dim(halves, 1 - core, 0, keepdims=False))

    share = hyper_in.shape[1]
    hidden = call(
        "hidden",
        hidden_body,
        jax.ShapeDtypeStruct((MP, task_count, share), jnp.bfloat16),
        (task_table, layer_table, hyper_in.T),
        (layer_index,),
        in_hbm,
    )
    hidden = exchange(hidden, "mp")

    sent, hidden, gen_other = lax.optimization_barrier(
        (spread(halves, given), hidden, swap_cores(gen_down))
    )
    gathered = exchange(sent, "mp", SAME_CORE)

    hidden = jnp.moveaxis(hidden, 0, 1).reshape(task_count, -1)
    generators = (gen_down, gen_up, gen_other)
    made = jnp.stack([matmul(hidden, generator).astype(jnp.bfloat16) for generator in generators])
    all_tasks, (wi_gate, wi_linear, wo_out) = doubling_gather(
        made, "dp", DP, (wi_gate, wi_linear, wo_out)
    )
    all_tasks = jnp.transpose(all_tasks, (5, 6, 4, 3, 2, 1, 0, 7))
    down, up, down_other = all_tasks.reshape(len(generators), task_count, width, R)

    gate, linear = wi_gate.T, wi_linear.T
    gate_other, linear_other, wo_other = swap_cores(gate), swap_cores(linear), swap_cores(wo_out)

    partial = ffn(
        gathered,
        norm_gain.reshape(1, features),
        (gate, gate_other),
        (linear, linear_other),
        (wo_out, wo_other),
    )
    parts = exchange(partial, "mp", SAME_CORE)
    mine, given, squeeze_part = squeeze(task_ids, parts, down, down_other)
    theirs = swap_cores(given)
    squeezed = exchange(relu_for_everyone(exchange(squeeze_part, "mp", SAME_CORE)), "mp")
    return expand(task_ids, tokens, mine, theirs, squeezed, up)


def solution(mesh):
    return jax.shard_map(
        per_device,
        mesh=mesh,
        in_specs=(
            P("dp", "mp"),
            P(),
            P(None, "mp"),
            P(None, "mp"),
            P("mp", None),
            P(),
            P(),
            P("dp"),
            P(),
            P(None, "mp"),
            P(None, ("mp", "dp")),
            P(None, ("mp", "dp")),
        ),
        out_specs=P("dp", "mp"),
        check_vma=False,
    )
```

```python
import jax
import jax.numpy as jnp
from jax import lax
from jax.experimental import pallas as pl
from jax.experimental.pallas import tpu as pltpu
from jax.sharding import PartitionSpec as P

R = 64
CORES = 2
CHIPS = 8
MP = CORES * CHIPS
SAME_CORE = [[chip * CORES + core for chip in range(CHIPS)] for core in range(CORES)]
VMEM = 32 * 1024 * 1024
FFN_TILE = 256


def matmul(left, right):
    return jnp.dot(left, right, preferred_element_type=jnp.float32)


def matmul_nt(left, right):
    return lax.dot_general(
        left, right, (((1,), (1,)), ((), ())), preferred_element_type=jnp.float32
    )


def exchange(pieces, axis, groups=None):
    return lax.all_to_all(
        pieces, axis, split_axis=0, concat_axis=0, axis_index_groups=groups, tiled=True
    )


def swap_cores(array):
    return lax.ppermute(array, "mp", [(i, i ^ 1) for i in range(MP)])


def doubling_gather(shard, axis, bits):
    index = lax.axis_index(axis)
    size = lax.axis_size(axis)
    held = shard
    for bit in bits:
        theirs = lax.ppermute(held, axis, [(i, i ^ bit) for i in range(size)])
        upper = (index & bit) != 0
        held = jnp.stack([jnp.where(upper, theirs, held), jnp.where(upper, held, theirs)])
    return held


def in_vmem(array):
    return pltpu.with_memory_space_constraint(array, pltpu.VMEM)


def in_hbm(array):
    return pltpu.with_memory_space_constraint(array, pltpu.HBM)


def whole(array):
    return pl.BlockSpec(memory_space=pltpu.VMEM)


def call(name, body, outs, arrays, scalars=(), place=in_vmem):
    return pl.pallas_call(
        body,
        out_shape=outs,
        in_specs=[pl.BlockSpec(memory_space=pltpu.SMEM) for _ in scalars] + [whole(a) for a in arrays],
        out_specs=jax.tree.map(lambda a: whole(a), outs),
        compiler_params=pltpu.CompilerParams(vmem_limit_bytes=VMEM),
        name=name,
    )(*scalars, *[place(a) for a in arrays])


def spread_body(tokens_ref, given_ref, out_ref, kept_ref, load_sem, sems):
    me = lax.axis_index("mp") % CORES
    load = pltpu.make_async_copy(tokens_ref.at[me], kept_ref, load_sem)
    load.start()
    copies = []
    for i in range(CHIPS):
        second = out_ref.at[CORES * i + 1 - me]
        copies.append(pltpu.make_async_copy(given_ref, second, sems.at[CHIPS + i]))
        copies[i].start()
    load.wait()
    for i in range(CHIPS):
        first = out_ref.at[CORES * i + me]
        copies.append(pltpu.make_async_copy(kept_ref, first, sems.at[i]))
        copies[CHIPS + i].start()
    for copy in copies:
        copy.wait()


def spread(halves, given):
    return pl.pallas_call(
        spread_body,
        out_shape=pltpu.HBM((MP, *given.shape), given.dtype),
        in_specs=[pl.BlockSpec(memory_space=pltpu.HBM), whole(given)],
        out_specs=pl.BlockSpec(memory_space=pltpu.HBM),
        scratch_shapes=[
            pltpu.VMEM(given.shape, given.dtype),
            pltpu.SemaphoreType.DMA(()),
            pltpu.SemaphoreType.DMA((MP,)),
        ],
        name="spread",
    )(in_hbm(halves), in_vmem(given))


def ffn_body(
    x_ref,
    gain_ref,
    gate_ref,
    gate_other_ref,
    linear_ref,
    linear_other_ref,
    wo_own_ref,
    wo_other_ref,
    out_ref,
    normed_ref,
    wi_ref,
    wo_ref,
    sums_ref,
    in_sems,
    out_sems,
):
    rows, width = x_ref.shape[1:]
    hid, features = wo_ref.shape
    own = hid // 2
    sides = [slice(0, features // 2), slice(features // 2, features)]
    placed = [
        (source.at[:, side], wi_ref.at[pl.ds(i * own, own), side])
        for side in sides
        for i, source in enumerate((gate_ref, gate_other_ref, linear_ref, linear_other_ref))
    ]
    placed += [
        (wo_own_ref, wo_ref.at[pl.ds(0, own)]),
        (wo_other_ref, wo_ref.at[pl.ds(own, own)]),
    ]
    loads = [pltpu.make_async_copy(a, b, in_sems.at[i]) for i, (a, b) in enumerate(placed)]
    for load in loads:
        load.start()
    gain = gain_ref[...].astype(jnp.float32)
    tiles = [pl.ds(k * FFN_TILE, FFN_TILE) for k in range(rows // FFN_TILE)]
    for tile in tiles:
        wide = jnp.concatenate([x_ref[i, tile] for i in range(MP)], axis=1).astype(jnp.float32)
        scale = lax.rsqrt(jnp.mean(wide * wide, axis=-1, keepdims=True) + 1e-06)
        normed_ref[tile] = (wide * scale * gain).astype(jnp.bfloat16)
    stores = []
    for k, tile in enumerate(tiles):
        if k == 0:
            for load in loads[:4]:
                load.wait()
            both = matmul_nt(normed_ref[tile, sides[0]], wi_ref[:, sides[0]])
            for load in loads[4:8]:
                load.wait()
            both = both + matmul_nt(normed_ref[tile, sides[1]], wi_ref[:, sides[1]])
        else:
            both = matmul_nt(normed_ref[tile], wi_ref[...])
        act = (jax.nn.gelu(both[:, :hid], approximate=True) * both[:, hid:]).astype(jnp.bfloat16)
        if k == 0:
            for load in loads[8:]:
                load.wait()
        for j, side in enumerate(sides):
            sums = matmul(act, wo_ref[:, side]).astype(jnp.bfloat16)
            blocks = slice(j * MP // 2, (j + 1) * MP // 2)
            for i in range(MP // 2):
                sums_ref[k, j * MP // 2 + i] = sums[:, i * width : (i + 1) * width]
            store = pltpu.make_async_copy(
                sums_ref.at[k, blocks], out_ref.at[blocks, tile], out_sems.at[2 * k + j]
            )
            store.start()
            stores.append(store)
    for store in stores:
        store.wait()


def ffn(x, gain, gates, linears, wos):
    rows, width = x.shape[1:]
    own, features = wos[0].shape
    tiles = rows // FFN_TILE
    weights = (*gates, *linears, *wos)
    hbm = pl.BlockSpec(memory_space=pltpu.HBM)
    return pl.pallas_call(
        ffn_body,
        out_shape=pltpu.HBM(x.shape, x.dtype),
        in_specs=[whole(x), whole(gain)] + [hbm] * len(weights),
        out_specs=hbm,
        scratch_shapes=[
            pltpu.VMEM((rows, features), x.dtype),
            pltpu.VMEM((4 * own, features), x.dtype),
            pltpu.VMEM((2 * own, features), x.dtype),
            pltpu.VMEM((tiles, MP, FFN_TILE, width), x.dtype),
            pltpu.SemaphoreType.DMA((10,)),
            pltpu.SemaphoreType.DMA((2 * tiles,)),
        ],
        compiler_params=pltpu.CompilerParams(vmem_limit_bytes=VMEM),
        name="ffn",
    )(in_vmem(x), in_vmem(gain), *[in_hbm(w) for w in weights])


def squeeze_body(
    ids_ref,
    parts_ref,
    down_ref,
    other_ref,
    kept_out,
    given_out,
    squeezed_out,
    kept_ref,
    given_ref,
    squeezed_ref,
    sems,
):
    rows = parts_ref.shape[1]
    seqs = ids_ref.shape[0]
    seq = rows * CORES // seqs
    me = lax.axis_index("mp") % CORES
    for s in range(rows // seq):
        tile = slice(s * seq, (s + 1) * seq)
        task = ids_ref[me * (rows // seq) + s]
        ffout = []
        for core in range(CORES):
            total = parts_ref[core, tile].astype(jnp.float32)
            for i in range(1, CHIPS):
                total = total + parts_ref[CORES * i + core, tile].astype(jnp.float32)
            ffout.append(total)
        kept = jnp.where(me == 0, ffout[0], ffout[1]).astype(jnp.bfloat16)
        given = jnp.where(me == 0, ffout[1], ffout[0]).astype(jnp.bfloat16)
        kept_ref[tile] = kept
        given_ref[tile] = given
        sums = (matmul(kept, down_ref[task]) + matmul(given, other_ref[task])).astype(jnp.bfloat16)
        packed = slice(s // 2 * seq, (s // 2 + 1) * seq)
        squeezed_ref[packed, s % 2 * R : (s % 2 + 1) * R] = sums
    stores = [pltpu.make_async_copy(squeezed_ref, squeezed_out.at[i], sems.at[i]) for i in range(MP)]
    stores.append(pltpu.make_async_copy(given_ref, given_out, sems.at[MP]))
    stores.append(pltpu.make_async_copy(kept_ref, kept_out, sems.at[MP + 1]))
    for store in stores:
        store.start()
    for store in stores:
        store.wait()


def squeeze(task_ids, parts, down, other):
    rows, width = parts.shape[1:]
    packed = (rows // 2, 2 * R)
    arrays = (parts, down, other)
    hbm = pl.BlockSpec(memory_space=pltpu.HBM)
    return pl.pallas_call(
        squeeze_body,
        out_shape=(
            pltpu.HBM((rows, width), parts.dtype),
            pltpu.HBM((rows, width), parts.dtype),
            pltpu.HBM((MP, *packed), parts.dtype),
        ),
        in_specs=[pl.BlockSpec(memory_space=pltpu.SMEM)] + [whole(a) for a in arrays],
        out_specs=(hbm, hbm, hbm),
        scratch_shapes=[
            pltpu.VMEM((rows, width), parts.dtype),
            pltpu.VMEM((rows, width), parts.dtype),
            pltpu.VMEM(packed, parts.dtype),
            pltpu.SemaphoreType.DMA((MP + 2,)),
        ],
        compiler_params=pltpu.CompilerParams(vmem_limit_bytes=VMEM),
        name="squeeze",
    )(task_ids, *[in_vmem(a) for a in arrays])


def expand_body(ids_ref, tokens_ref, mine_ref, theirs_ref, parts_ref, up_ref, out_ref):
    seqs = ids_ref.shape[0]
    seq = tokens_ref.shape[0] // seqs
    per_core = seqs // CORES
    me = lax.axis_index("mp") % CORES
    for core in range(CORES):
        total = parts_ref[core].astype(jnp.float32)
        for i in range(1, CHIPS):
            total = total + parts_ref[CORES * i + core].astype(jnp.float32)
        squeezed = jnp.maximum(total, 0.0).astype(jnp.bfloat16)
        for j in range(per_core):
            s = core * per_core + j
            tile = slice(s * seq, (s + 1) * seq)
            part = slice(j * seq, (j + 1) * seq)
            left = squeezed[j // 2 * seq : (j // 2 + 1) * seq, j % 2 * R : (j % 2 + 1) * R]
            expand = matmul_nt(left, up_ref[ids_ref[s]])
            ffout = jnp.where(me == core, mine_ref[part], theirs_ref[part])
            total = tokens_ref[tile].astype(jnp.float32) + ffout.astype(jnp.float32) + expand
            out_ref[tile] = total.astype(jnp.bfloat16)


def expand(task_ids, tokens, mine, theirs, parts, up):
    out = jax.ShapeDtypeStruct(tokens.shape, tokens.dtype)
    return call("expand", expand_body, out, (tokens, mine, theirs, parts, up), (task_ids,))


def hidden_body(layer_ref, task_table_ref, layer_table_ref, hyper_in_ref, out_ref):
    task_table = task_table_ref[...]
    row = layer_table_ref[pl.ds(layer_ref[0], 1)]
    embed = jnp.concatenate([task_table, jnp.broadcast_to(row, task_table.shape)], axis=1)
    hidden = jnp.maximum(matmul_nt(embed.astype(jnp.bfloat16), hyper_in_ref[...]), 0.0)
    for i in range(MP):
        out_ref[i] = hidden.astype(jnp.bfloat16)


def per_device(
    tokens,
    norm_gain,
    wi_gate,
    wi_linear,
    wo_out,
    task_table,
    layer_table,
    task_ids,
    layer_index,
    hyper_in,
    gen_down,
    gen_up,
):
    tok_dev, width = tokens.shape
    features = width * MP
    half = tok_dev // CORES
    core = lax.axis_index("mp") % CORES
    task_count = task_table.shape[0]

    halves = tokens.reshape(CORES, half, width)
    given = swap_cores(lax.dynamic_index_in_dim(halves, 1 - core, 0, keepdims=False))

    hidden = call(
        "hidden",
        hidden_body,
        jax.ShapeDtypeStruct((MP, task_count, hyper_in.shape[1]), jnp.bfloat16),
        (task_table, layer_table, hyper_in.T),
        (layer_index,),
        in_hbm,
    )
    hidden = exchange(hidden, "mp")
    hidden, sent, gen_given, gate, linear, wo = lax.optimization_barrier(
        (hidden, spread(halves, given), gen_down, wi_gate.T, wi_linear.T, wo_out)
    )
    gathered = exchange(sent, "mp", SAME_CORE)

    gate_other, linear_other, wo_other = swap_cores(gate), swap_cores(linear), swap_cores(wo)

    hidden = jnp.moveaxis(hidden, 0, 1).reshape(task_count, -1)
    generators = (gen_down, gen_up, swap_cores(gen_given))
    made = jnp.stack([matmul(hidden, generator).astype(jnp.bfloat16) for generator in generators])
    all_tasks = doubling_gather(made, "dp", (16, 1, 8, 4, 2))
    all_tasks = jnp.transpose(all_tasks, (5, 6, 4, 2, 1, 0, 3, 7))
    down, up, down_other = all_tasks.reshape(len(generators), task_count, width, R)

    partial = ffn(
        gathered,
        norm_gain.reshape(1, features),
        (gate, gate_other),
        (linear, linear_other),
        (wo, wo_other),
    )
    parts = exchange(partial, "mp", SAME_CORE)
    mine, given, squeeze_part = squeeze(task_ids, parts, down, down_other)
    theirs = swap_cores(given)
    return expand(task_ids, tokens, mine, theirs, exchange(squeeze_part, "mp"), up)


def solution(mesh):
    return jax.shard_map(
        per_device,
        mesh=mesh,
        in_specs=(
            P("dp", "mp"),
            P(),
            P(None, "mp"),
            P(None, "mp"),
            P("mp", None),
            P(),
            P(),
            P("dp"),
            P(),
            P(None, "mp"),
            P(None, ("mp", "dp")),
            P(None, ("mp", "dp")),
        ),
        out_specs=P("dp", "mp"),
        check_vma=False,
    )
```

```python
import jax
import jax.numpy as jnp
from jax import lax
from jax.experimental import pallas as pl
from jax.experimental.pallas import tpu as pltpu
from jax.sharding import PartitionSpec as P

R = 64
CORES = 2
CHIPS = 8
MP = CORES * CHIPS
SAME_CORE = [[chip * CORES + core for chip in range(CHIPS)] for core in range(CORES)]
VMEM = 32 * 1024 * 1024
FFN_TILE = 256


def matmul(left, right):
    return jnp.dot(left, right, preferred_element_type=jnp.float32)


def matmul_nt(left, right):
    return lax.dot_general(
        left, right, (((1,), (1,)), ((), ())), preferred_element_type=jnp.float32
    )


def exchange(pieces, axis, groups=None):
    return lax.all_to_all(
        pieces, axis, split_axis=0, concat_axis=0, axis_index_groups=groups, tiled=True
    )


def swap_cores(array):
    return lax.ppermute(array, "mp", [(i, i ^ 1) for i in range(MP)])


def doubling_gather(shard, axis, bits):
    index = lax.axis_index(axis)
    size = lax.axis_size(axis)
    held = shard
    for bit in bits:
        theirs = lax.ppermute(held, axis, [(i, i ^ bit) for i in range(size)])
        upper = (index & bit) != 0
        held = jnp.stack([jnp.where(upper, theirs, held), jnp.where(upper, held, theirs)])
    return held


def in_vmem(array):
    return pltpu.with_memory_space_constraint(array, pltpu.VMEM)


def in_hbm(array):
    return pltpu.with_memory_space_constraint(array, pltpu.HBM)


def whole(array):
    return pl.BlockSpec(memory_space=pltpu.VMEM)


def call(name, body, outs, arrays, scalars=(), place=in_vmem):
    return pl.pallas_call(
        body,
        out_shape=outs,
        in_specs=[pl.BlockSpec(memory_space=pltpu.SMEM) for _ in scalars] + [whole(a) for a in arrays],
        out_specs=jax.tree.map(lambda a: whole(a), outs),
        compiler_params=pltpu.CompilerParams(vmem_limit_bytes=VMEM),
        name=name,
    )(*scalars, *[place(a) for a in arrays])


def spread_body(tokens_ref, given_ref, out_ref, kept_ref, load_sem, sems):
    me = lax.axis_index("mp") % CORES
    load = pltpu.make_async_copy(tokens_ref.at[me], kept_ref, load_sem)
    load.start()
    copies = []
    for i in range(CHIPS):
        second = out_ref.at[CORES * i + 1 - me]
        copies.append(pltpu.make_async_copy(given_ref, second, sems.at[CHIPS + i]))
        copies[i].start()
    load.wait()
    for i in range(CHIPS):
        first = out_ref.at[CORES * i + me]
        copies.append(pltpu.make_async_copy(kept_ref, first, sems.at[i]))
        copies[CHIPS + i].start()
    for copy in copies:
        copy.wait()


def spread(halves, given):
    return pl.pallas_call(
        spread_body,
        out_shape=pltpu.HBM((MP, *given.shape), given.dtype),
        in_specs=[pl.BlockSpec(memory_space=pltpu.HBM), whole(given)],
        out_specs=pl.BlockSpec(memory_space=pltpu.HBM),
        scratch_shapes=[
            pltpu.VMEM(given.shape, given.dtype),
            pltpu.SemaphoreType.DMA(()),
            pltpu.SemaphoreType.DMA((MP,)),
        ],
        name="spread",
    )(in_hbm(halves), in_vmem(given))


def ffn_body(
    x_ref,
    gain_ref,
    gate_ref,
    gate_other_ref,
    linear_ref,
    linear_other_ref,
    wo_own_ref,
    wo_other_ref,
    out_ref,
    normed_ref,
    wi_ref,
    wo_ref,
    sums_ref,
    in_sems,
    out_sems,
):
    rows, width = x_ref.shape[1:]
    hid, features = wo_ref.shape
    own = hid // 2
    sides = [slice(0, features // 2), slice(features // 2, features)]
    placed = [
        (source.at[:, side], wi_ref.at[pl.ds(i * own, own), side])
        for side in sides
        for i, source in enumerate((gate_ref, gate_other_ref, linear_ref, linear_other_ref))
    ]
    placed += [
        (wo_own_ref, wo_ref.at[pl.ds(0, own)]),
        (wo_other_ref, wo_ref.at[pl.ds(own, own)]),
    ]
    loads = [pltpu.make_async_copy(a, b, in_sems.at[i]) for i, (a, b) in enumerate(placed)]
    for load in loads:
        load.start()
    gain = gain_ref[...].astype(jnp.float32)
    tiles = [pl.ds(k * FFN_TILE, FFN_TILE) for k in range(rows // FFN_TILE)]
    for tile in tiles:
        wide = jnp.concatenate([x_ref[i, tile] for i in range(MP)], axis=1).astype(jnp.float32)
        scale = lax.rsqrt(jnp.mean(wide * wide, axis=-1, keepdims=True) + 1e-06)
        normed_ref[tile] = (wide * scale * gain).astype(jnp.bfloat16)
    stores = []
    for k, tile in enumerate(tiles):
        if k == 0:
            for load in loads[:4]:
                load.wait()
            both = matmul_nt(normed_ref[tile, sides[0]], wi_ref[:, sides[0]])
            for load in loads[4:8]:
                load.wait()
            both = both + matmul_nt(normed_ref[tile, sides[1]], wi_ref[:, sides[1]])
        else:
            both = matmul_nt(normed_ref[tile], wi_ref[...])
        act = (jax.nn.gelu(both[:, :hid], approximate=True) * both[:, hid:]).astype(jnp.bfloat16)
        if k == 0:
            for load in loads[8:]:
                load.wait()
        for j, side in enumerate(sides):
            sums = matmul(act, wo_ref[:, side]).astype(jnp.bfloat16)
            blocks = slice(j * MP // 2, (j + 1) * MP // 2)
            for i in range(MP // 2):
                sums_ref[k, j * MP // 2 + i] = sums[:, i * width : (i + 1) * width]
            store = pltpu.make_async_copy(
                sums_ref.at[k, blocks], out_ref.at[blocks, tile], out_sems.at[2 * k + j]
            )
            store.start()
            stores.append(store)
    for store in stores:
        store.wait()


def ffn(x, gain, gates, linears, wos):
    rows, width = x.shape[1:]
    own, features = wos[0].shape
    tiles = rows // FFN_TILE
    weights = (*gates, *linears, *wos)
    hbm = pl.BlockSpec(memory_space=pltpu.HBM)
    return pl.pallas_call(
        ffn_body,
        out_shape=pltpu.HBM(x.shape, x.dtype),
        in_specs=[whole(x), whole(gain)] + [hbm] * len(weights),
        out_specs=hbm,
        scratch_shapes=[
            pltpu.VMEM((rows, features), x.dtype),
            pltpu.VMEM((4 * own, features), x.dtype),
            pltpu.VMEM((2 * own, features), x.dtype),
            pltpu.VMEM((tiles, MP, FFN_TILE, width), x.dtype),
            pltpu.SemaphoreType.DMA((10,)),
            pltpu.SemaphoreType.DMA((2 * tiles,)),
        ],
        compiler_params=pltpu.CompilerParams(vmem_limit_bytes=VMEM),
        name="ffn",
    )(in_vmem(x), in_vmem(gain), *[in_hbm(w) for w in weights])


def squeeze_body(
    ids_ref,
    parts_ref,
    down_ref,
    other_ref,
    kept_out,
    given_out,
    squeezed_out,
    kept_ref,
    given_ref,
    squeezed_ref,
    sems,
):
    rows = parts_ref.shape[1]
    seqs = ids_ref.shape[0]
    seq = rows * CORES // seqs
    me = lax.axis_index("mp") % CORES
    for s in range(rows // seq):
        tile = slice(s * seq, (s + 1) * seq)
        task = ids_ref[me * (rows // seq) + s]
        ffout = []
        for core in range(CORES):
            total = parts_ref[core, tile].astype(jnp.float32)
            for i in range(1, CHIPS):
                total = total + parts_ref[CORES * i + core, tile].astype(jnp.float32)
            ffout.append(total)
        kept = jnp.where(me == 0, ffout[0], ffout[1]).astype(jnp.bfloat16)
        given = jnp.where(me == 0, ffout[1], ffout[0]).astype(jnp.bfloat16)
        kept_ref[tile] = kept
        given_ref[tile] = given
        sums = (matmul(kept, down_ref[task]) + matmul(given, other_ref[task])).astype(jnp.bfloat16)
        packed = slice(s // 2 * seq, (s // 2 + 1) * seq)
        squeezed_ref[packed, s % 2 * R : (s % 2 + 1) * R] = sums
    stores = [pltpu.make_async_copy(squeezed_ref, squeezed_out.at[i], sems.at[i]) for i in range(CHIPS)]
    stores.append(pltpu.make_async_copy(given_ref, given_out, sems.at[CHIPS]))
    stores.append(pltpu.make_async_copy(kept_ref, kept_out, sems.at[CHIPS + 1]))
    for store in stores:
        store.start()
    for store in stores:
        store.wait()


def squeeze(task_ids, parts, down, other):
    rows, width = parts.shape[1:]
    packed = (rows // 2, 2 * R)
    arrays = (parts, down, other)
    hbm = pl.BlockSpec(memory_space=pltpu.HBM)
    return pl.pallas_call(
        squeeze_body,
        out_shape=(
            pltpu.HBM((rows, width), parts.dtype),
            pltpu.HBM((rows, width), parts.dtype),
            pltpu.HBM((CHIPS, *packed), parts.dtype),
        ),
        in_specs=[pl.BlockSpec(memory_space=pltpu.SMEM)] + [whole(a) for a in arrays],
        out_specs=(hbm, hbm, hbm),
        scratch_shapes=[
            pltpu.VMEM((rows, width), parts.dtype),
            pltpu.VMEM((rows, width), parts.dtype),
            pltpu.VMEM(packed, parts.dtype),
            pltpu.SemaphoreType.DMA((CHIPS + 2,)),
        ],
        compiler_params=pltpu.CompilerParams(vmem_limit_bytes=VMEM),
        name="squeeze",
    )(task_ids, *[in_vmem(a) for a in arrays])


def relu_body(parts_ref, out_ref):
    total = parts_ref[0].astype(jnp.float32)
    for i in range(1, CHIPS):
        total = total + parts_ref[i].astype(jnp.float32)
    out_ref[...] = jnp.maximum(total, 0.0).astype(jnp.bfloat16)


def relu_sum(parts):
    out = jax.ShapeDtypeStruct(parts.shape[1:], parts.dtype)
    return call("relu_sum", relu_body, out, (parts,))


def expand_body(
    ids_ref, tokens_ref, mine_ref, theirs_ref, squeezed_ref, their_squeezed_ref, up_ref, out_ref
):
    seqs = ids_ref.shape[0]
    seq = tokens_ref.shape[0] // seqs
    per_core = seqs // CORES
    me = lax.axis_index("mp") % CORES
    for core in range(CORES):
        squeezed = jnp.where(me == core, squeezed_ref[...], their_squeezed_ref[...])
        for j in range(per_core):
            s = core * per_core + j
            tile = slice(s * seq, (s + 1) * seq)
            part = slice(j * seq, (j + 1) * seq)
            left = squeezed[j // 2 * seq : (j // 2 + 1) * seq, j % 2 * R : (j % 2 + 1) * R]
            expand = matmul_nt(left, up_ref[ids_ref[s]])
            ffout = jnp.where(me == core, mine_ref[part], theirs_ref[part])
            total = tokens_ref[tile].astype(jnp.float32) + ffout.astype(jnp.float32) + expand
            out_ref[tile] = total.astype(jnp.bfloat16)


def expand(task_ids, tokens, mine, theirs, squeezed, their_squeezed, up):
    out = jax.ShapeDtypeStruct(tokens.shape, tokens.dtype)
    arrays = (tokens, mine, theirs, squeezed, their_squeezed, up)
    return call("expand", expand_body, out, arrays, (task_ids,))


def hidden_body(layer_ref, task_table_ref, layer_table_ref, hyper_in_ref, out_ref):
    task_table = task_table_ref[...]
    row = layer_table_ref[pl.ds(layer_ref[0], 1)]
    embed = jnp.concatenate([task_table, jnp.broadcast_to(row, task_table.shape)], axis=1)
    hidden = jnp.maximum(matmul_nt(embed.astype(jnp.bfloat16), hyper_in_ref[...]), 0.0)
    for i in range(MP):
        out_ref[i] = hidden.astype(jnp.bfloat16)


def per_device(
    tokens,
    norm_gain,
    wi_gate,
    wi_linear,
    wo_out,
    task_table,
    layer_table,
    task_ids,
    layer_index,
    hyper_in,
    gen_down,
    gen_up,
):
    tok_dev, width = tokens.shape
    features = width * MP
    half = tok_dev // CORES
    core = lax.axis_index("mp") % CORES
    task_count = task_table.shape[0]

    halves = tokens.reshape(CORES, half, width)
    given = swap_cores(lax.dynamic_index_in_dim(halves, 1 - core, 0, keepdims=False))

    hidden = call(
        "hidden",
        hidden_body,
        jax.ShapeDtypeStruct((MP, task_count, hyper_in.shape[1]), jnp.bfloat16),
        (task_table, layer_table, hyper_in.T),
        (layer_index,),
        in_hbm,
    )

    hidden, gate, linear, wo, gen_down = lax.optimization_barrier(
        (hidden, wi_gate.T, wi_linear.T, wo_out, gen_down)
    )
    hidden = exchange(hidden, "mp")
    others = [swap_cores(w) for w in (gate, linear, wo, gen_down)]
    hidden, sent, others = lax.optimization_barrier((hidden, spread(halves, given), others))
    gate_other, linear_other, wo_other, gen_other = others
    gathered = exchange(sent, "mp", SAME_CORE)

    hidden = jnp.moveaxis(hidden, 0, 1).reshape(task_count, -1)
    generators = (gen_down, gen_up, gen_other)
    made = jnp.stack([matmul(hidden, generator).astype(jnp.bfloat16) for generator in generators])
    all_tasks = doubling_gather(made, "dp", (16, 1, 8, 4, 2))
    all_tasks = jnp.transpose(all_tasks, (5, 6, 4, 2, 1, 0, 3, 7))
    down, up, down_other = all_tasks.reshape(len(generators), task_count, width, R)

    partial = ffn(
        gathered,
        norm_gain.reshape(1, features),
        (gate, gate_other),
        (linear, linear_other),
        (wo, wo_other),
    )
    parts = exchange(partial, "mp", SAME_CORE)
    mine, given, squeeze_part = squeeze(task_ids, parts, down, down_other)
    theirs = swap_cores(given)
    squeezed = relu_sum(exchange(squeeze_part, "mp", SAME_CORE))
    return expand(task_ids, tokens, mine, theirs, squeezed, swap_cores(squeezed), up)


def solution(mesh):
    return jax.shard_map(
        per_device,
        mesh=mesh,
        in_specs=(
            P("dp", "mp"),
            P(),
            P(None, "mp"),
            P(None, "mp"),
            P("mp", None),
            P(),
            P(),
            P("dp"),
            P(),
            P(None, "mp"),
            P(None, ("mp", "dp")),
            P(None, ("mp", "dp")),
        ),
        out_specs=P("dp", "mp"),
        check_vma=False,
    )
```

```python
import jax
import jax.numpy as jnp
from jax import lax
from jax.experimental import pallas as pl
from jax.experimental.pallas import tpu as pltpu
from jax.sharding import PartitionSpec as P

R = 64
CORES = 2
CHIPS = 8
MP = CORES * CHIPS
SAME_CORE = [[chip * CORES + core for chip in range(CHIPS)] for core in range(CORES)]
VMEM = 32 * 1024 * 1024
FFN_TILE = 256


def matmul(left, right):
    return jnp.dot(left, right, preferred_element_type=jnp.float32)


def matmul_nt(left, right):
    return lax.dot_general(
        left, right, (((1,), (1,)), ((), ())), preferred_element_type=jnp.float32
    )


def exchange(pieces, axis, groups=None):
    return lax.all_to_all(
        pieces, axis, split_axis=0, concat_axis=0, axis_index_groups=groups, tiled=True
    )


def swap_cores(array):
    return lax.ppermute(array, "mp", [(i, i ^ 1) for i in range(MP)])


def doubling_gather(shard, axis, bits, later):
    index = lax.axis_index(axis)
    size = lax.axis_size(axis)
    held = shard
    released = []
    for bit, array in zip(bits, later, strict=True):
        held, array = lax.optimization_barrier((held, array))
        released.append(array)
        theirs = lax.ppermute(held, axis, [(i, i ^ bit) for i in range(size)])
        upper = (index & bit) != 0
        held = jnp.stack([jnp.where(upper, theirs, held), jnp.where(upper, held, theirs)])
    return held, released


def in_vmem(array):
    return pltpu.with_memory_space_constraint(array, pltpu.VMEM)


def in_hbm(array):
    return pltpu.with_memory_space_constraint(array, pltpu.HBM)


def whole(array):
    return pl.BlockSpec(memory_space=pltpu.VMEM)


def call(name, body, outs, arrays, scalars=(), place=in_vmem):
    return pl.pallas_call(
        body,
        out_shape=outs,
        in_specs=[pl.BlockSpec(memory_space=pltpu.SMEM) for _ in scalars] + [whole(a) for a in arrays],
        out_specs=jax.tree.map(lambda a: whole(a), outs),
        compiler_params=pltpu.CompilerParams(vmem_limit_bytes=VMEM),
        name=name,
    )(*scalars, *[place(a) for a in arrays])


def spread_body(tokens_ref, given_ref, out_ref, kept_ref, load_sem, sems):
    me = lax.axis_index("mp") % CORES
    load = pltpu.make_async_copy(tokens_ref.at[me], kept_ref, load_sem)
    load.start()
    copies = []
    for i in range(CHIPS):
        second = out_ref.at[CORES * i + 1 - me]
        copies.append(pltpu.make_async_copy(given_ref, second, sems.at[CHIPS + i]))
        copies[i].start()
    load.wait()
    for i in range(CHIPS):
        first = out_ref.at[CORES * i + me]
        copies.append(pltpu.make_async_copy(kept_ref, first, sems.at[i]))
        copies[CHIPS + i].start()
    for copy in copies:
        copy.wait()


def spread(halves, given):
    return pl.pallas_call(
        spread_body,
        out_shape=pltpu.HBM((MP, *given.shape), given.dtype),
        in_specs=[pl.BlockSpec(memory_space=pltpu.HBM), whole(given)],
        out_specs=pl.BlockSpec(memory_space=pltpu.HBM),
        scratch_shapes=[
            pltpu.VMEM(given.shape, given.dtype),
            pltpu.SemaphoreType.DMA(()),
            pltpu.SemaphoreType.DMA((MP,)),
        ],
        name="spread",
    )(in_hbm(halves), in_vmem(given))


def ffn_body(
    x_ref,
    gain_ref,
    gate_ref,
    gate_other_ref,
    linear_ref,
    linear_other_ref,
    wo_own_ref,
    wo_other_ref,
    out_ref,
    normed_ref,
    wi_ref,
    wo_ref,
    sums_ref,
    in_sems,
    out_sems,
):
    rows, width = x_ref.shape[1:]
    hid, features = wo_ref.shape
    own = hid // 2
    sides = [slice(0, features // 2), slice(features // 2, features)]
    placed = [
        (source.at[:, side], wi_ref.at[pl.ds(i * own, own), side])
        for side in sides
        for i, source in enumerate((gate_ref, gate_other_ref, linear_ref, linear_other_ref))
    ]
    placed += [
        (wo_own_ref, wo_ref.at[pl.ds(0, own)]),
        (wo_other_ref, wo_ref.at[pl.ds(own, own)]),
    ]
    loads = [pltpu.make_async_copy(a, b, in_sems.at[i]) for i, (a, b) in enumerate(placed)]
    for load in loads:
        load.start()
    gain = gain_ref[...].astype(jnp.float32)
    tiles = [pl.ds(k * FFN_TILE, FFN_TILE) for k in range(rows // FFN_TILE)]
    for tile in tiles:
        wide = jnp.concatenate([x_ref[i, tile] for i in range(MP)], axis=1).astype(jnp.float32)
        scale = lax.rsqrt(jnp.mean(wide * wide, axis=-1, keepdims=True) + 1e-06)
        normed_ref[tile] = (wide * scale * gain).astype(jnp.bfloat16)
    stores = []
    for k, tile in enumerate(tiles):
        if k == 0:
            for load in loads[:4]:
                load.wait()
            both = matmul_nt(normed_ref[tile, sides[0]], wi_ref[:, sides[0]])
            for load in loads[4:8]:
                load.wait()
            both = both + matmul_nt(normed_ref[tile, sides[1]], wi_ref[:, sides[1]])
        else:
            both = matmul_nt(normed_ref[tile], wi_ref[...])
        act = (jax.nn.gelu(both[:, :hid], approximate=True) * both[:, hid:]).astype(jnp.bfloat16)
        if k == 0:
            for load in loads[8:]:
                load.wait()
        for j, side in enumerate(sides):
            sums = matmul(act, wo_ref[:, side]).astype(jnp.bfloat16)
            blocks = slice(j * MP // 2, (j + 1) * MP // 2)
            for i in range(MP // 2):
                sums_ref[k, j * MP // 2 + i] = sums[:, i * width : (i + 1) * width]
            store = pltpu.make_async_copy(
                sums_ref.at[k, blocks], out_ref.at[blocks, tile], out_sems.at[2 * k + j]
            )
            store.start()
            stores.append(store)
    for store in stores:
        store.wait()


def ffn(x, gain, gates, linears, wos):
    rows, width = x.shape[1:]
    own, features = wos[0].shape
    tiles = rows // FFN_TILE
    weights = (*gates, *linears, *wos)
    hbm = pl.BlockSpec(memory_space=pltpu.HBM)
    return pl.pallas_call(
        ffn_body,
        out_shape=pltpu.HBM(x.shape, x.dtype),
        in_specs=[whole(x), whole(gain)] + [hbm] * len(weights),
        out_specs=hbm,
        scratch_shapes=[
            pltpu.VMEM((rows, features), x.dtype),
            pltpu.VMEM((4 * own, features), x.dtype),
            pltpu.VMEM((2 * own, features), x.dtype),
            pltpu.VMEM((tiles, MP, FFN_TILE, width), x.dtype),
            pltpu.SemaphoreType.DMA((10,)),
            pltpu.SemaphoreType.DMA((2 * tiles,)),
        ],
        compiler_params=pltpu.CompilerParams(vmem_limit_bytes=VMEM),
        name="ffn",
    )(in_vmem(x), in_vmem(gain), *[in_hbm(w) for w in weights])


def squeeze_body(
    ids_ref,
    parts_ref,
    down_ref,
    other_ref,
    kept_out,
    given_out,
    squeezed_out,
    kept_ref,
    given_ref,
    squeezed_ref,
    sems,
):
    rows = parts_ref.shape[1]
    seqs = ids_ref.shape[0]
    seq = rows * CORES // seqs
    me = lax.axis_index("mp") % CORES
    for s in range(rows // seq):
        tile = slice(s * seq, (s + 1) * seq)
        task = ids_ref[me * (rows // seq) + s]
        ffout = []
        for core in range(CORES):
            total = parts_ref[core, tile].astype(jnp.float32)
            for i in range(1, CHIPS):
                total = total + parts_ref[CORES * i + core, tile].astype(jnp.float32)
            ffout.append(total)
        kept = jnp.where(me == 0, ffout[0], ffout[1]).astype(jnp.bfloat16)
        given = jnp.where(me == 0, ffout[1], ffout[0]).astype(jnp.bfloat16)
        kept_ref[tile] = kept
        given_ref[tile] = given
        sums = (matmul(kept, down_ref[task]) + matmul(given, other_ref[task])).astype(jnp.bfloat16)
        packed = slice(s // 2 * seq, (s // 2 + 1) * seq)
        squeezed_ref[packed, s % 2 * R : (s % 2 + 1) * R] = sums
    stores = [pltpu.make_async_copy(squeezed_ref, squeezed_out.at[i], sems.at[i]) for i in range(CHIPS)]
    stores.append(pltpu.make_async_copy(given_ref, given_out, sems.at[CHIPS]))
    stores.append(pltpu.make_async_copy(kept_ref, kept_out, sems.at[CHIPS + 1]))
    for store in stores:
        store.start()
    for store in stores:
        store.wait()


def squeeze(task_ids, parts, down, other):
    rows, width = parts.shape[1:]
    packed = (rows // 2, 2 * R)
    arrays = (parts, down, other)
    hbm = pl.BlockSpec(memory_space=pltpu.HBM)
    return pl.pallas_call(
        squeeze_body,
        out_shape=(
            pltpu.HBM((rows, width), parts.dtype),
            pltpu.HBM((rows, width), parts.dtype),
            pltpu.HBM((CHIPS, *packed), parts.dtype),
        ),
        in_specs=[pl.BlockSpec(memory_space=pltpu.SMEM)] + [whole(a) for a in arrays],
        out_specs=(hbm, hbm, hbm),
        scratch_shapes=[
            pltpu.VMEM((rows, width), parts.dtype),
            pltpu.VMEM((rows, width), parts.dtype),
            pltpu.VMEM(packed, parts.dtype),
            pltpu.SemaphoreType.DMA((CHIPS + 2,)),
        ],
        compiler_params=pltpu.CompilerParams(vmem_limit_bytes=VMEM),
        name="squeeze",
    )(task_ids, *[in_vmem(a) for a in arrays])


def relu_body(parts_ref, out_ref):
    total = parts_ref[0].astype(jnp.float32)
    for i in range(1, CHIPS):
        total = total + parts_ref[i].astype(jnp.float32)
    out_ref[...] = jnp.maximum(total, 0.0).astype(jnp.bfloat16)


def relu_sum(parts):
    out = jax.ShapeDtypeStruct(parts.shape[1:], parts.dtype)
    return call("relu_sum", relu_body, out, (parts,))


def expand_body(
    ids_ref, tokens_ref, mine_ref, theirs_ref, squeezed_ref, their_squeezed_ref, up_ref, out_ref
):
    seqs = ids_ref.shape[0]
    seq = tokens_ref.shape[0] // seqs
    per_core = seqs // CORES
    me = lax.axis_index("mp") % CORES
    for core in range(CORES):
        squeezed = jnp.where(me == core, squeezed_ref[...], their_squeezed_ref[...])
        for j in range(per_core):
            s = core * per_core + j
            tile = slice(s * seq, (s + 1) * seq)
            part = slice(j * seq, (j + 1) * seq)
            left = squeezed[j // 2 * seq : (j // 2 + 1) * seq, j % 2 * R : (j % 2 + 1) * R]
            expand = matmul_nt(left, up_ref[ids_ref[s]])
            ffout = jnp.where(me == core, mine_ref[part], theirs_ref[part])
            total = tokens_ref[tile].astype(jnp.float32) + ffout.astype(jnp.float32) + expand
            out_ref[tile] = total.astype(jnp.bfloat16)


def expand(task_ids, tokens, mine, theirs, squeezed, their_squeezed, up):
    out = jax.ShapeDtypeStruct(tokens.shape, tokens.dtype)
    arrays = (tokens, mine, theirs, squeezed, their_squeezed, up)
    return call("expand", expand_body, out, arrays, (task_ids,))


def hidden_body(layer_ref, task_table_ref, layer_table_ref, hyper_in_ref, out_ref):
    task_table = task_table_ref[...]
    row = layer_table_ref[pl.ds(layer_ref[0], 1)]
    embed = jnp.concatenate([task_table, jnp.broadcast_to(row, task_table.shape)], axis=1)
    hidden = jnp.maximum(matmul_nt(embed.astype(jnp.bfloat16), hyper_in_ref[...]), 0.0)
    for i in range(MP):
        out_ref[i] = hidden.astype(jnp.bfloat16)


def per_device(
    tokens,
    norm_gain,
    wi_gate,
    wi_linear,
    wo_out,
    task_table,
    layer_table,
    task_ids,
    layer_index,
    hyper_in,
    gen_down,
    gen_up,
):
    tok_dev, width = tokens.shape
    features = width * MP
    half = tok_dev // CORES
    core = lax.axis_index("mp") % CORES
    task_count = task_table.shape[0]

    halves = tokens.reshape(CORES, half, width)
    given = swap_cores(lax.dynamic_index_in_dim(halves, 1 - core, 0, keepdims=False))

    hidden = call(
        "hidden",
        hidden_body,
        jax.ShapeDtypeStruct((MP, task_count, hyper_in.shape[1]), jnp.bfloat16),
        (task_table, layer_table, hyper_in.T),
        (layer_index,),
        in_hbm,
    )
    hidden = exchange(hidden, "mp")
    hidden, sent = lax.optimization_barrier((hidden, spread(halves, given)))
    gathered = exchange(sent, "mp", SAME_CORE)

    hidden = jnp.moveaxis(hidden, 0, 1).reshape(task_count, -1)
    made = jnp.stack(
        [matmul(hidden, gen_down).astype(jnp.bfloat16), matmul(hidden, gen_up).astype(jnp.bfloat16)]
    )
    near, (gate, linear, wo) = doubling_gather(
        made, "dp", (1, 2, 4), (wi_gate.T, wi_linear.T, wo_out)
    )
    gate_other, linear_other, wo_other = swap_cores(gate), swap_cores(linear), swap_cores(wo)
    gathered, near = lax.optimization_barrier((gathered, near))
    far = lax.axis_size("dp") // 8
    strided = [[8 * i + place for i in range(far)] for place in range(8)]
    near = near.reshape(1, 8, *made.shape)
    all_tasks = exchange(jnp.broadcast_to(near, (far, *near.shape[1:])), "dp", strided)

    partial = ffn(
        gathered,
        norm_gain.reshape(1, features),
        (gate, gate_other),
        (linear, linear_other),
        (wo, wo_other),
    )
    partial, all_tasks = lax.optimization_barrier((partial, all_tasks))
    parts = exchange(partial, "mp", SAME_CORE)
    adapters = jnp.transpose(all_tasks, (2, 3, 0, 1, 4)).reshape(2, task_count, width, R)
    down, up = adapters[0], adapters[1]
    mine, given, squeeze_part = squeeze(task_ids, parts, down, swap_cores(down))
    theirs = swap_cores(given)
    squeezed = relu_sum(exchange(squeeze_part, "mp", SAME_CORE))
    return expand(task_ids, tokens, mine, theirs, squeezed, swap_cores(squeezed), up)


def solution(mesh):
    return jax.shard_map(
        per_device,
        mesh=mesh,
        in_specs=(
            P("dp", "mp"),
            P(),
            P(None, "mp"),
            P(None, "mp"),
            P("mp", None),
            P(),
            P(),
            P("dp"),
            P(),
            P(None, "mp"),
            P(None, ("mp", "dp")),
            P(None, ("mp", "dp")),
        ),
        out_specs=P("dp", "mp"),
        check_vma=False,
    )
```

```python
import jax
import jax.numpy as jnp
from jax import lax
from jax.experimental import pallas as pl
from jax.experimental.pallas import tpu as pltpu
from jax.sharding import PartitionSpec as P

R = 64
CORES = 2
CHIPS = 8
MP = CORES * CHIPS
SAME_CORE = [[chip * CORES + core for chip in range(CHIPS)] for core in range(CORES)]
VMEM = 32 * 1024 * 1024
FFN_TILE = 256


def matmul(left, right):
    return jnp.dot(left, right, preferred_element_type=jnp.float32)


def matmul_nt(left, right):
    return lax.dot_general(
        left, right, (((1,), (1,)), ((), ())), preferred_element_type=jnp.float32
    )


def exchange(pieces, axis, groups=None):
    return lax.all_to_all(
        pieces, axis, split_axis=0, concat_axis=0, axis_index_groups=groups, tiled=True
    )


def swap_cores(array):
    return lax.ppermute(array, "mp", [(i, i ^ 1) for i in range(MP)])


def doubling_gather(shard, axis, bits):
    index = lax.axis_index(axis)
    size = lax.axis_size(axis)
    held = shard
    for bit in bits:
        theirs = lax.ppermute(held, axis, [(i, i ^ bit) for i in range(size)])
        upper = (index & bit) != 0
        held = jnp.stack([jnp.where(upper, theirs, held), jnp.where(upper, held, theirs)])
    return held


def in_vmem(array):
    return pltpu.with_memory_space_constraint(array, pltpu.VMEM)


def in_hbm(array):
    return pltpu.with_memory_space_constraint(array, pltpu.HBM)


def whole(array):
    return pl.BlockSpec(memory_space=pltpu.VMEM)


def call(name, body, outs, arrays, scalars=(), place=in_vmem):
    return pl.pallas_call(
        body,
        out_shape=outs,
        in_specs=[pl.BlockSpec(memory_space=pltpu.SMEM) for _ in scalars] + [whole(a) for a in arrays],
        out_specs=jax.tree.map(lambda a: whole(a), outs),
        compiler_params=pltpu.CompilerParams(vmem_limit_bytes=VMEM),
        name=name,
    )(*scalars, *[place(a) for a in arrays])


def spread_body(tokens_ref, given_ref, out_ref, kept_ref, load_sem, sems):
    me = lax.axis_index("mp") % CORES
    load = pltpu.make_async_copy(tokens_ref.at[me], kept_ref, load_sem)
    load.start()
    copies = []
    for i in range(CHIPS):
        second = out_ref.at[CORES * i + 1 - me]
        copies.append(pltpu.make_async_copy(given_ref, second, sems.at[CHIPS + i]))
        copies[i].start()
    load.wait()
    for i in range(CHIPS):
        first = out_ref.at[CORES * i + me]
        copies.append(pltpu.make_async_copy(kept_ref, first, sems.at[i]))
        copies[CHIPS + i].start()
    for copy in copies:
        copy.wait()


def spread(halves, given):
    return pl.pallas_call(
        spread_body,
        out_shape=pltpu.HBM((MP, *given.shape), given.dtype),
        in_specs=[pl.BlockSpec(memory_space=pltpu.HBM), whole(given)],
        out_specs=pl.BlockSpec(memory_space=pltpu.HBM),
        scratch_shapes=[
            pltpu.VMEM(given.shape, given.dtype),
            pltpu.SemaphoreType.DMA(()),
            pltpu.SemaphoreType.DMA((MP,)),
        ],
        name="spread",
    )(in_hbm(halves), in_vmem(given))


def ffn_body(
    x_ref,
    gain_ref,
    gate_ref,
    gate_other_ref,
    linear_ref,
    linear_other_ref,
    wo_own_ref,
    wo_other_ref,
    out_ref,
    normed_ref,
    wi_ref,
    wo_ref,
    sums_ref,
    in_sems,
    out_sems,
):
    rows, width = x_ref.shape[1:]
    hid, features = wo_ref.shape
    own = hid // 2
    sides = [slice(0, features // 2), slice(features // 2, features)]
    placed = [
        (source.at[:, side], wi_ref.at[pl.ds(i * own, own), side])
        for side in sides
        for i, source in enumerate((gate_ref, gate_other_ref, linear_ref, linear_other_ref))
    ]
    placed += [
        (wo_own_ref, wo_ref.at[pl.ds(0, own)]),
        (wo_other_ref, wo_ref.at[pl.ds(own, own)]),
    ]
    loads = [pltpu.make_async_copy(a, b, in_sems.at[i]) for i, (a, b) in enumerate(placed)]
    for load in loads:
        load.start()
    gain = gain_ref[...].astype(jnp.float32)
    tiles = [pl.ds(k * FFN_TILE, FFN_TILE) for k in range(rows // FFN_TILE)]
    for tile in tiles:
        wide = jnp.concatenate([x_ref[i, tile] for i in range(MP)], axis=1).astype(jnp.float32)
        scale = lax.rsqrt(jnp.mean(wide * wide, axis=-1, keepdims=True) + 1e-06)
        normed_ref[tile] = (wide * scale * gain).astype(jnp.bfloat16)
    stores = []
    for k, tile in enumerate(tiles):
        if k == 0:
            for load in loads[:4]:
                load.wait()
            both = matmul_nt(normed_ref[tile, sides[0]], wi_ref[:, sides[0]])
            for load in loads[4:8]:
                load.wait()
            both = both + matmul_nt(normed_ref[tile, sides[1]], wi_ref[:, sides[1]])
        else:
            both = matmul_nt(normed_ref[tile], wi_ref[...])
        act = (jax.nn.gelu(both[:, :hid], approximate=True) * both[:, hid:]).astype(jnp.bfloat16)
        if k == 0:
            for load in loads[8:]:
                load.wait()
        for j, side in enumerate(sides):
            sums = matmul(act, wo_ref[:, side]).astype(jnp.bfloat16)
            blocks = slice(j * MP // 2, (j + 1) * MP // 2)
            for i in range(MP // 2):
                sums_ref[k, j * MP // 2 + i] = sums[:, i * width : (i + 1) * width]
            store = pltpu.make_async_copy(
                sums_ref.at[k, blocks], out_ref.at[blocks, tile], out_sems.at[2 * k + j]
            )
            store.start()
            stores.append(store)
    for store in stores:
        store.wait()


def ffn(x, gain, gates, linears, wos):
    rows, width = x.shape[1:]
    own, features = wos[0].shape
    tiles = rows // FFN_TILE
    weights = (*gates, *linears, *wos)
    hbm = pl.BlockSpec(memory_space=pltpu.HBM)
    return pl.pallas_call(
        ffn_body,
        out_shape=pltpu.HBM(x.shape, x.dtype),
        in_specs=[whole(x), whole(gain)] + [hbm] * len(weights),
        out_specs=hbm,
        scratch_shapes=[
            pltpu.VMEM((rows, features), x.dtype),
            pltpu.VMEM((4 * own, features), x.dtype),
            pltpu.VMEM((2 * own, features), x.dtype),
            pltpu.VMEM((tiles, MP, FFN_TILE, width), x.dtype),
            pltpu.SemaphoreType.DMA((10,)),
            pltpu.SemaphoreType.DMA((2 * tiles,)),
        ],
        compiler_params=pltpu.CompilerParams(vmem_limit_bytes=VMEM),
        name="ffn",
    )(in_vmem(x), in_vmem(gain), *[in_hbm(w) for w in weights])


def squeeze_body(
    ids_ref,
    parts_ref,
    down_ref,
    other_ref,
    kept_out,
    given_out,
    squeezed_out,
    kept_ref,
    given_ref,
    squeezed_ref,
    sems,
):
    rows = parts_ref.shape[1]
    seqs = ids_ref.shape[0]
    seq = rows * CORES // seqs
    me = lax.axis_index("mp") % CORES
    for s in range(rows // seq):
        tile = slice(s * seq, (s + 1) * seq)
        task = ids_ref[me * (rows // seq) + s]
        ffout = []
        for core in range(CORES):
            total = parts_ref[core, tile].astype(jnp.float32)
            for i in range(1, CHIPS):
                total = total + parts_ref[CORES * i + core, tile].astype(jnp.float32)
            ffout.append(total)
        kept = jnp.where(me == 0, ffout[0], ffout[1]).astype(jnp.bfloat16)
        given = jnp.where(me == 0, ffout[1], ffout[0]).astype(jnp.bfloat16)
        kept_ref[tile] = kept
        given_ref[tile] = given
        sums = (matmul(kept, down_ref[task]) + matmul(given, other_ref[task])).astype(jnp.bfloat16)
        packed = slice(s // 2 * seq, (s // 2 + 1) * seq)
        squeezed_ref[packed, s % 2 * R : (s % 2 + 1) * R] = sums
    stores = [pltpu.make_async_copy(squeezed_ref, squeezed_out.at[i], sems.at[i]) for i in range(CHIPS)]
    stores.append(pltpu.make_async_copy(given_ref, given_out, sems.at[CHIPS]))
    stores.append(pltpu.make_async_copy(kept_ref, kept_out, sems.at[CHIPS + 1]))
    for store in stores:
        store.start()
    for store in stores:
        store.wait()


def squeeze(task_ids, parts, down, other):
    rows, width = parts.shape[1:]
    packed = (rows // 2, 2 * R)
    arrays = (parts, down, other)
    hbm = pl.BlockSpec(memory_space=pltpu.HBM)
    return pl.pallas_call(
        squeeze_body,
        out_shape=(
            pltpu.HBM((rows, width), parts.dtype),
            pltpu.HBM((rows, width), parts.dtype),
            pltpu.HBM((CHIPS, *packed), parts.dtype),
        ),
        in_specs=[pl.BlockSpec(memory_space=pltpu.SMEM)] + [whole(a) for a in arrays],
        out_specs=(hbm, hbm, hbm),
        scratch_shapes=[
            pltpu.VMEM((rows, width), parts.dtype),
            pltpu.VMEM((rows, width), parts.dtype),
            pltpu.VMEM(packed, parts.dtype),
            pltpu.SemaphoreType.DMA((CHIPS + 2,)),
        ],
        compiler_params=pltpu.CompilerParams(vmem_limit_bytes=VMEM),
        name="squeeze",
    )(task_ids, *[in_vmem(a) for a in arrays])


def relu_body(parts_ref, out_ref):
    total = parts_ref[0].astype(jnp.float32)
    for i in range(1, CHIPS):
        total = total + parts_ref[i].astype(jnp.float32)
    out_ref[...] = jnp.maximum(total, 0.0).astype(jnp.bfloat16)


def relu_sum(parts):
    out = jax.ShapeDtypeStruct(parts.shape[1:], parts.dtype)
    return call("relu_sum", relu_body, out, (parts,))


def expand_body(
    ids_ref, tokens_ref, mine_ref, theirs_ref, squeezed_ref, their_squeezed_ref, up_ref, out_ref
):
    seqs = ids_ref.shape[0]
    seq = tokens_ref.shape[0] // seqs
    per_core = seqs // CORES
    me = lax.axis_index("mp") % CORES
    for core in range(CORES):
        squeezed = jnp.where(me == core, squeezed_ref[...], their_squeezed_ref[...])
        for j in range(per_core):
            s = core * per_core + j
            tile = slice(s * seq, (s + 1) * seq)
            part = slice(j * seq, (j + 1) * seq)
            left = squeezed[j // 2 * seq : (j // 2 + 1) * seq, j % 2 * R : (j % 2 + 1) * R]
            expand = matmul_nt(left, up_ref[ids_ref[s]])
            ffout = jnp.where(me == core, mine_ref[part], theirs_ref[part])
            total = tokens_ref[tile].astype(jnp.float32) + ffout.astype(jnp.float32) + expand
            out_ref[tile] = total.astype(jnp.bfloat16)


def expand(task_ids, tokens, mine, theirs, squeezed, their_squeezed, up):
    out = jax.ShapeDtypeStruct(tokens.shape, tokens.dtype)
    arrays = (tokens, mine, theirs, squeezed, their_squeezed, up)
    return call("expand", expand_body, out, arrays, (task_ids,))


def hidden_body(layer_ref, task_table_ref, layer_table_ref, hyper_in_ref, out_ref):
    task_table = task_table_ref[...]
    row = layer_table_ref[pl.ds(layer_ref[0], 1)]
    embed = jnp.concatenate([task_table, jnp.broadcast_to(row, task_table.shape)], axis=1)
    hidden = jnp.maximum(matmul_nt(embed.astype(jnp.bfloat16), hyper_in_ref[...]), 0.0)
    for i in range(MP):
        out_ref[i] = hidden.astype(jnp.bfloat16)


def per_device(
    tokens,
    norm_gain,
    wi_gate,
    wi_linear,
    wo_out,
    task_table,
    layer_table,
    task_ids,
    layer_index,
    hyper_in,
    gen_down,
    gen_up,
):
    tok_dev, width = tokens.shape
    features = width * MP
    half = tok_dev // CORES
    core = lax.axis_index("mp") % CORES
    task_count = task_table.shape[0]

    halves = tokens.reshape(CORES, half, width)
    given = swap_cores(lax.dynamic_index_in_dim(halves, 1 - core, 0, keepdims=False))

    hidden = call(
        "hidden",
        hidden_body,
        jax.ShapeDtypeStruct((MP, task_count, hyper_in.shape[1]), jnp.bfloat16),
        (task_table, layer_table, hyper_in.T),
        (layer_index,),
        in_hbm,
    )

    hidden = exchange(hidden, "mp")
    hidden, sent, gate, linear, wo, gen_down = lax.optimization_barrier(
        (hidden, spread(halves, given), wi_gate.T, wi_linear.T, wo_out, gen_down)
    )
    others = [swap_cores(w) for w in (gate, linear, wo, gen_down)]
    gate_other, linear_other, wo_other, gen_other = others
    gathered = exchange(sent, "mp", SAME_CORE)

    hidden = jnp.moveaxis(hidden, 0, 1).reshape(task_count, -1)
    generators = (gen_down, gen_up, gen_other)
    made = jnp.stack([matmul(hidden, generator).astype(jnp.bfloat16) for generator in generators])
    all_tasks = doubling_gather(made, "dp", (16, 1, 8, 4, 2))
    all_tasks = jnp.transpose(all_tasks, (5, 6, 4, 2, 1, 0, 3, 7))
    down, up, down_other = all_tasks.reshape(len(generators), task_count, width, R)

    partial = ffn(
        gathered,
        norm_gain.reshape(1, features),
        (gate, gate_other),
        (linear, linear_other),
        (wo, wo_other),
    )
    parts = exchange(partial, "mp", SAME_CORE)
    mine, given, squeeze_part = squeeze(task_ids, parts, down, down_other)
    theirs = swap_cores(given)
    squeezed = relu_sum(exchange(squeeze_part, "mp", SAME_CORE))
    return expand(task_ids, tokens, mine, theirs, squeezed, swap_cores(squeezed), up)


def solution(mesh):
    return jax.shard_map(
        per_device,
        mesh=mesh,
        in_specs=(
            P("dp", "mp"),
            P(),
            P(None, "mp"),
            P(None, "mp"),
            P("mp", None),
            P(),
            P(),
            P("dp"),
            P(),
            P(None, "mp"),
            P(None, ("mp", "dp")),
            P(None, ("mp", "dp")),
        ),
        out_specs=P("dp", "mp"),
        check_vma=False,
    )
```

```python
import jax
import jax.numpy as jnp
from jax import lax
from jax.experimental import pallas as pl
from jax.experimental.pallas import tpu as pltpu
from jax.sharding import PartitionSpec as P

R = 64
CORES = 2
CHIPS = 8
MP = CORES * CHIPS
SAME_CORE = [[chip * CORES + core for chip in range(CHIPS)] for core in range(CORES)]
VMEM = 32 * 1024 * 1024
FFN_TILE = 256


def matmul(left, right):
    return jnp.dot(left, right, preferred_element_type=jnp.float32)


def matmul_nt(left, right):
    return lax.dot_general(
        left, right, (((1,), (1,)), ((), ())), preferred_element_type=jnp.float32
    )


def exchange(pieces, axis, groups=None):
    return lax.all_to_all(
        pieces, axis, split_axis=0, concat_axis=0, axis_index_groups=groups, tiled=True
    )


def swap_cores(array):
    return lax.ppermute(array, "mp", [(i, i ^ 1) for i in range(MP)])


def doubling_gather(shard, axis, bits):
    index = lax.axis_index(axis)
    size = lax.axis_size(axis)
    held = shard
    for bit in bits:
        theirs = lax.ppermute(held, axis, [(i, i ^ bit) for i in range(size)])
        upper = (index & bit) != 0
        held = jnp.stack([jnp.where(upper, theirs, held), jnp.where(upper, held, theirs)])
    return held


def in_vmem(array):
    return pltpu.with_memory_space_constraint(array, pltpu.VMEM)


def in_hbm(array):
    return pltpu.with_memory_space_constraint(array, pltpu.HBM)


def whole(array):
    return pl.BlockSpec(memory_space=pltpu.VMEM)


def call(name, body, outs, arrays, scalars=(), place=in_vmem):
    return pl.pallas_call(
        body,
        out_shape=outs,
        in_specs=[pl.BlockSpec(memory_space=pltpu.SMEM) for _ in scalars] + [whole(a) for a in arrays],
        out_specs=jax.tree.map(lambda a: whole(a), outs),
        compiler_params=pltpu.CompilerParams(vmem_limit_bytes=VMEM),
        name=name,
    )(*scalars, *[place(a) for a in arrays])


def spread_body(tokens_ref, given_ref, out_ref, kept_ref, load_sem, sems):
    me = lax.axis_index("mp") % CORES
    load = pltpu.make_async_copy(tokens_ref.at[me], kept_ref, load_sem)
    load.start()
    copies = []
    for i in range(CHIPS):
        second = out_ref.at[CORES * i + 1 - me]
        copies.append(pltpu.make_async_copy(given_ref, second, sems.at[CHIPS + i]))
        copies[i].start()
    load.wait()
    for i in range(CHIPS):
        first = out_ref.at[CORES * i + me]
        copies.append(pltpu.make_async_copy(kept_ref, first, sems.at[i]))
        copies[CHIPS + i].start()
    for copy in copies:
        copy.wait()


def spread(halves, given):
    return pl.pallas_call(
        spread_body,
        out_shape=pltpu.HBM((MP, *given.shape), given.dtype),
        in_specs=[pl.BlockSpec(memory_space=pltpu.HBM), whole(given)],
        out_specs=pl.BlockSpec(memory_space=pltpu.HBM),
        scratch_shapes=[
            pltpu.VMEM(given.shape, given.dtype),
            pltpu.SemaphoreType.DMA(()),
            pltpu.SemaphoreType.DMA((MP,)),
        ],
        name="spread",
    )(in_hbm(halves), in_vmem(given))


def ffn_body(
    x_ref,
    gain_ref,
    gate_ref,
    gate_other_ref,
    linear_ref,
    linear_other_ref,
    wo_own_ref,
    wo_other_ref,
    out_ref,
    normed_ref,
    wi_ref,
    wo_ref,
    sums_ref,
    in_sems,
    out_sems,
):
    rows, width = x_ref.shape[1:]
    hid, features = wo_ref.shape
    own = hid // 2
    sides = [slice(0, features // 2), slice(features // 2, features)]
    placed = [
        (source.at[:, side], wi_ref.at[pl.ds(i * own, own), side])
        for side in sides
        for i, source in enumerate((gate_ref, gate_other_ref, linear_ref, linear_other_ref))
    ]
    placed += [
        (wo_own_ref, wo_ref.at[pl.ds(0, own)]),
        (wo_other_ref, wo_ref.at[pl.ds(own, own)]),
    ]
    loads = [pltpu.make_async_copy(a, b, in_sems.at[i]) for i, (a, b) in enumerate(placed)]
    for load in loads:
        load.start()
    gain = gain_ref[...].astype(jnp.float32)
    tiles = [pl.ds(k * FFN_TILE, FFN_TILE) for k in range(rows // FFN_TILE)]
    for tile in tiles:
        wide = jnp.concatenate([x_ref[i, tile] for i in range(MP)], axis=1).astype(jnp.float32)
        scale = lax.rsqrt(jnp.mean(wide * wide, axis=-1, keepdims=True) + 1e-06)
        normed_ref[tile] = (wide * scale * gain).astype(jnp.bfloat16)
    stores = []
    for k, tile in enumerate(tiles):
        if k == 0:
            for load in loads[:4]:
                load.wait()
            both = matmul_nt(normed_ref[tile, sides[0]], wi_ref[:, sides[0]])
            for load in loads[4:8]:
                load.wait()
            both = both + matmul_nt(normed_ref[tile, sides[1]], wi_ref[:, sides[1]])
        else:
            both = matmul_nt(normed_ref[tile], wi_ref[...])
        act = (jax.nn.gelu(both[:, :hid], approximate=True) * both[:, hid:]).astype(jnp.bfloat16)
        if k == 0:
            for load in loads[8:]:
                load.wait()
        for j, side in enumerate(sides):
            sums = matmul(act, wo_ref[:, side]).astype(jnp.bfloat16)
            blocks = slice(j * MP // 2, (j + 1) * MP // 2)
            for i in range(MP // 2):
                sums_ref[k, j * MP // 2 + i] = sums[:, i * width : (i + 1) * width]
            store = pltpu.make_async_copy(
                sums_ref.at[k, blocks], out_ref.at[blocks, tile], out_sems.at[2 * k + j]
            )
            store.start()
            stores.append(store)
    for store in stores:
        store.wait()


def ffn(x, gain, gates, linears, wos):
    rows, width = x.shape[1:]
    own, features = wos[0].shape
    tiles = rows // FFN_TILE
    weights = (*gates, *linears, *wos)
    hbm = pl.BlockSpec(memory_space=pltpu.HBM)
    return pl.pallas_call(
        ffn_body,
        out_shape=pltpu.HBM(x.shape, x.dtype),
        in_specs=[whole(x), whole(gain)] + [hbm] * len(weights),
        out_specs=hbm,
        scratch_shapes=[
            pltpu.VMEM((rows, features), x.dtype),
            pltpu.VMEM((4 * own, features), x.dtype),
            pltpu.VMEM((2 * own, features), x.dtype),
            pltpu.VMEM((tiles, MP, FFN_TILE, width), x.dtype),
            pltpu.SemaphoreType.DMA((10,)),
            pltpu.SemaphoreType.DMA((2 * tiles,)),
        ],
        compiler_params=pltpu.CompilerParams(vmem_limit_bytes=VMEM),
        name="ffn",
    )(in_vmem(x), in_vmem(gain), *[in_hbm(w) for w in weights])


def squeeze_body(
    ids_ref,
    parts_ref,
    down_ref,
    other_ref,
    kept_out,
    given_out,
    squeezed_out,
    kept_ref,
    given_ref,
    squeezed_ref,
    sems,
):
    rows = parts_ref.shape[1]
    seqs = ids_ref.shape[0]
    seq = rows * CORES // seqs
    me = lax.axis_index("mp") % CORES
    for s in range(rows // seq):
        tile = slice(s * seq, (s + 1) * seq)
        task = ids_ref[me * (rows // seq) + s]
        ffout = []
        for core in range(CORES):
            total = parts_ref[core, tile].astype(jnp.float32)
            for i in range(1, CHIPS):
                total = total + parts_ref[CORES * i + core, tile].astype(jnp.float32)
            ffout.append(total)
        kept = jnp.where(me == 0, ffout[0], ffout[1]).astype(jnp.bfloat16)
        given = jnp.where(me == 0, ffout[1], ffout[0]).astype(jnp.bfloat16)
        kept_ref[tile] = kept
        given_ref[tile] = given
        sums = (matmul(kept, down_ref[task]) + matmul(given, other_ref[task])).astype(jnp.bfloat16)
        packed = slice(s // 2 * seq, (s // 2 + 1) * seq)
        squeezed_ref[packed, s % 2 * R : (s % 2 + 1) * R] = sums
    stores = [pltpu.make_async_copy(squeezed_ref, squeezed_out.at[i], sems.at[i]) for i in range(CHIPS)]
    stores.append(pltpu.make_async_copy(given_ref, given_out, sems.at[CHIPS]))
    stores.append(pltpu.make_async_copy(kept_ref, kept_out, sems.at[CHIPS + 1]))
    for store in stores:
        store.start()
    for store in stores:
        store.wait()


def squeeze(task_ids, parts, down, other):
    rows, width = parts.shape[1:]
    packed = (rows // 2, 2 * R)
    arrays = (parts, down, other)
    hbm = pl.BlockSpec(memory_space=pltpu.HBM)
    return pl.pallas_call(
        squeeze_body,
        out_shape=(
            pltpu.HBM((rows, width), parts.dtype),
            pltpu.HBM((rows, width), parts.dtype),
            pltpu.HBM((CHIPS, *packed), parts.dtype),
        ),
        in_specs=[pl.BlockSpec(memory_space=pltpu.SMEM)] + [whole(a) for a in arrays],
        out_specs=(hbm, hbm, hbm),
        scratch_shapes=[
            pltpu.VMEM((rows, width), parts.dtype),
            pltpu.VMEM((rows, width), parts.dtype),
            pltpu.VMEM(packed, parts.dtype),
            pltpu.SemaphoreType.DMA((CHIPS + 2,)),
        ],
        compiler_params=pltpu.CompilerParams(vmem_limit_bytes=VMEM),
        name="squeeze",
    )(task_ids, *[in_vmem(a) for a in arrays])


def relu_body(parts_ref, out_ref):
    total = parts_ref[0].astype(jnp.float32)
    for i in range(1, CHIPS):
        total = total + parts_ref[i].astype(jnp.float32)
    out_ref[...] = jnp.maximum(total, 0.0).astype(jnp.bfloat16)


def relu_sum(parts):
    out = jax.ShapeDtypeStruct(parts.shape[1:], parts.dtype)
    return call("relu_sum", relu_body, out, (parts,))


def expand_body(
    ids_ref, tokens_ref, mine_ref, theirs_ref, squeezed_ref, their_squeezed_ref, up_ref, out_ref
):
    seqs = ids_ref.shape[0]
    seq = tokens_ref.shape[0] // seqs
    per_core = seqs // CORES
    me = lax.axis_index("mp") % CORES
    for core in range(CORES):
        squeezed = jnp.where(me == core, squeezed_ref[...], their_squeezed_ref[...])
        for j in range(per_core):
            s = core * per_core + j
            tile = slice(s * seq, (s + 1) * seq)
            part = slice(j * seq, (j + 1) * seq)
            left = squeezed[j // 2 * seq : (j // 2 + 1) * seq, j % 2 * R : (j % 2 + 1) * R]
            expand = matmul_nt(left, up_ref[ids_ref[s]])
            ffout = jnp.where(me == core, mine_ref[part], theirs_ref[part])
            total = tokens_ref[tile].astype(jnp.float32) + ffout.astype(jnp.float32) + expand
            out_ref[tile] = total.astype(jnp.bfloat16)


def expand(task_ids, tokens, mine, theirs, squeezed, their_squeezed, up):
    out = jax.ShapeDtypeStruct(tokens.shape, tokens.dtype)
    arrays = (tokens, mine, theirs, squeezed, their_squeezed, up)
    return call("expand", expand_body, out, arrays, (task_ids,))


def hidden_body(layer_ref, task_table_ref, layer_table_ref, hyper_in_ref, out_ref):
    task_table = task_table_ref[...]
    row = layer_table_ref[pl.ds(layer_ref[0], 1)]
    embed = jnp.concatenate([task_table, jnp.broadcast_to(row, task_table.shape)], axis=1)
    hidden = jnp.maximum(matmul_nt(embed.astype(jnp.bfloat16), hyper_in_ref[...]), 0.0)
    for i in range(MP):
        out_ref[i] = hidden.astype(jnp.bfloat16)


def per_device(
    tokens,
    norm_gain,
    wi_gate,
    wi_linear,
    wo_out,
    task_table,
    layer_table,
    task_ids,
    layer_index,
    hyper_in,
    gen_down,
    gen_up,
):
    tok_dev, width = tokens.shape
    features = width * MP
    half = tok_dev // CORES
    core = lax.axis_index("mp") % CORES
    task_count = task_table.shape[0]

    halves = tokens.reshape(CORES, half, width)
    given = swap_cores(lax.dynamic_index_in_dim(halves, 1 - core, 0, keepdims=False))

    hidden = call(
        "hidden",
        hidden_body,
        jax.ShapeDtypeStruct((MP, task_count, hyper_in.shape[1]), jnp.bfloat16),
        (task_table, layer_table, hyper_in.T),
        (layer_index,),
        in_hbm,
    )

    hidden = exchange(hidden, "mp")
    hidden, sent, gate, linear, wo = lax.optimization_barrier(
        (hidden, spread(halves, given), wi_gate.T, wi_linear.T, wo_out)
    )
    gate_other, linear_other, wo_other = [swap_cores(w) for w in (gate, linear, wo)]
    gathered = exchange(sent, "mp", SAME_CORE)

    hidden = jnp.moveaxis(hidden, 0, 1).reshape(task_count, -1)
    made_down, made_up = [
        matmul(hidden, generator).astype(jnp.bfloat16) for generator in (gen_down, gen_up)
    ]
    made = jnp.stack([made_down, swap_cores(made_down), made_up])
    most = doubling_gather(made, "dp", (16, 1, 8, 4))
    downs = doubling_gather(most[:, :, :, :, :2], "dp", (2,))
    downs = jnp.transpose(downs, (5, 6, 4, 2, 1, 0, 3, 7))
    down, down_other = downs.reshape(2, task_count, width, R)
    ups = doubling_gather(most[:, :, :, :, 2], "dp", (2,))
    up = jnp.transpose(ups, (5, 4, 2, 1, 0, 3, 6)).reshape(task_count, width, R)

    partial = ffn(
        gathered,
        norm_gain.reshape(1, features),
        (gate, gate_other),
        (linear, linear_other),
        (wo, wo_other),
    )
    parts = exchange(partial, "mp", SAME_CORE)
    mine, given, squeeze_part = squeeze(task_ids, parts, down, down_other)
    theirs = swap_cores(given)
    squeezed = relu_sum(exchange(squeeze_part, "mp", SAME_CORE))
    return expand(task_ids, tokens, mine, theirs, squeezed, swap_cores(squeezed), up)


def solution(mesh):
    return jax.shard_map(
        per_device,
        mesh=mesh,
        in_specs=(
            P("dp", "mp"),
            P(),
            P(None, "mp"),
            P(None, "mp"),
            P("mp", None),
            P(),
            P(),
            P("dp"),
            P(),
            P(None, "mp"),
            P(None, ("mp", "dp")),
            P(None, ("mp", "dp")),
        ),
        out_specs=P("dp", "mp"),
        check_vma=False,
    )
```

```python
import jax
import jax.numpy as jnp
from jax import lax
from jax.experimental import pallas as pl
from jax.experimental.pallas import tpu as pltpu
from jax.sharding import PartitionSpec as P

R = 64
CORES = 2
CHIPS = 8
MP = CORES * CHIPS
SAME_CORE = [[chip * CORES + core for chip in range(CHIPS)] for core in range(CORES)]
VMEM = 32 * 1024 * 1024
FFN_TILE = 256


def matmul(left, right):
    return jnp.dot(left, right, preferred_element_type=jnp.float32)


def matmul_nt(left, right):
    return lax.dot_general(
        left, right, (((1,), (1,)), ((), ())), preferred_element_type=jnp.float32
    )


def exchange(pieces, axis, groups=None):
    return lax.all_to_all(
        pieces, axis, split_axis=0, concat_axis=0, axis_index_groups=groups, tiled=True
    )


def swap_cores(array):
    return lax.ppermute(array, "mp", [(i, i ^ 1) for i in range(MP)])


def doubling_gather(shard, axis, bits):
    index = lax.axis_index(axis)
    size = lax.axis_size(axis)
    held = shard
    for bit in bits:
        theirs = lax.ppermute(held, axis, [(i, i ^ bit) for i in range(size)])
        upper = (index & bit) != 0
        held = jnp.stack([jnp.where(upper, theirs, held), jnp.where(upper, held, theirs)])
    return held


def in_vmem(array):
    return pltpu.with_memory_space_constraint(array, pltpu.VMEM)


def in_hbm(array):
    return pltpu.with_memory_space_constraint(array, pltpu.HBM)


def whole(array):
    return pl.BlockSpec(memory_space=pltpu.VMEM)


def call(name, body, outs, arrays, scalars=(), place=in_vmem):
    return pl.pallas_call(
        body,
        out_shape=outs,
        in_specs=[pl.BlockSpec(memory_space=pltpu.SMEM) for _ in scalars] + [whole(a) for a in arrays],
        out_specs=jax.tree.map(lambda a: whole(a), outs),
        compiler_params=pltpu.CompilerParams(vmem_limit_bytes=VMEM),
        name=name,
    )(*scalars, *[place(a) for a in arrays])


def spread_body(tokens_ref, given_ref, out_ref, kept_ref, load_sem, sems):
    me = lax.axis_index("mp") % CORES
    load = pltpu.make_async_copy(tokens_ref.at[me], kept_ref, load_sem)
    load.start()
    copies = []
    for i in range(CHIPS):
        second = out_ref.at[CORES * i + 1 - me]
        copies.append(pltpu.make_async_copy(given_ref, second, sems.at[CHIPS + i]))
        copies[i].start()
    load.wait()
    for i in range(CHIPS):
        first = out_ref.at[CORES * i + me]
        copies.append(pltpu.make_async_copy(kept_ref, first, sems.at[i]))
        copies[CHIPS + i].start()
    for copy in copies:
        copy.wait()


def spread(halves, given):
    return pl.pallas_call(
        spread_body,
        out_shape=pltpu.HBM((MP, *given.shape), given.dtype),
        in_specs=[pl.BlockSpec(memory_space=pltpu.HBM), whole(given)],
        out_specs=pl.BlockSpec(memory_space=pltpu.HBM),
        scratch_shapes=[
            pltpu.VMEM(given.shape, given.dtype),
            pltpu.SemaphoreType.DMA(()),
            pltpu.SemaphoreType.DMA((MP,)),
        ],
        name="spread",
    )(in_hbm(halves), in_vmem(given))


def ffn_body(
    x_ref,
    gain_ref,
    gate_ref,
    gate_other_ref,
    linear_ref,
    linear_other_ref,
    wo_own_ref,
    wo_other_ref,
    out_ref,
    normed_ref,
    wi_ref,
    wo_ref,
    sums_ref,
    in_sems,
    out_sems,
):
    rows, width = x_ref.shape[1:]
    hid, features = wo_ref.shape
    own = hid // 2
    sides = [slice(0, features // 2), slice(features // 2, features)]
    placed = [
        (source.at[:, side], wi_ref.at[pl.ds(i * own, own), side])
        for side in sides
        for i, source in enumerate((gate_ref, gate_other_ref, linear_ref, linear_other_ref))
    ]
    placed += [
        (wo_own_ref, wo_ref.at[pl.ds(0, own)]),
        (wo_other_ref, wo_ref.at[pl.ds(own, own)]),
    ]
    loads = [pltpu.make_async_copy(a, b, in_sems.at[i]) for i, (a, b) in enumerate(placed)]
    for load in loads:
        load.start()
    gain = gain_ref[...].astype(jnp.float32)
    tiles = [pl.ds(k * FFN_TILE, FFN_TILE) for k in range(rows // FFN_TILE)]
    for tile in tiles:
        wide = jnp.concatenate([x_ref[i, tile] for i in range(MP)], axis=1).astype(jnp.float32)
        scale = lax.rsqrt(jnp.mean(wide * wide, axis=-1, keepdims=True) + 1e-06)
        normed_ref[tile] = (wide * scale * gain).astype(jnp.bfloat16)
    stores = []
    for k, tile in enumerate(tiles):
        if k == 0:
            for load in loads[:4]:
                load.wait()
            both = matmul_nt(normed_ref[tile, sides[0]], wi_ref[:, sides[0]])
            for load in loads[4:8]:
                load.wait()
            both = both + matmul_nt(normed_ref[tile, sides[1]], wi_ref[:, sides[1]])
        else:
            both = matmul_nt(normed_ref[tile], wi_ref[...])
        act = (jax.nn.gelu(both[:, :hid], approximate=True) * both[:, hid:]).astype(jnp.bfloat16)
        if k == 0:
            for load in loads[8:]:
                load.wait()
        for j, side in enumerate(sides):
            sums = matmul(act, wo_ref[:, side]).astype(jnp.bfloat16)
            blocks = slice(j * MP // 2, (j + 1) * MP // 2)
            for i in range(MP // 2):
                sums_ref[k, j * MP // 2 + i] = sums[:, i * width : (i + 1) * width]
            store = pltpu.make_async_copy(
                sums_ref.at[k, blocks], out_ref.at[blocks, tile], out_sems.at[2 * k + j]
            )
            store.start()
            stores.append(store)
    for store in stores:
        store.wait()


def ffn(x, gain, gates, linears, wos):
    rows, width = x.shape[1:]
    own, features = wos[0].shape
    tiles = rows // FFN_TILE
    weights = (*gates, *linears, *wos)
    hbm = pl.BlockSpec(memory_space=pltpu.HBM)
    return pl.pallas_call(
        ffn_body,
        out_shape=pltpu.HBM(x.shape, x.dtype),
        in_specs=[whole(x), whole(gain)] + [hbm] * len(weights),
        out_specs=hbm,
        scratch_shapes=[
            pltpu.VMEM((rows, features), x.dtype),
            pltpu.VMEM((4 * own, features), x.dtype),
            pltpu.VMEM((2 * own, features), x.dtype),
            pltpu.VMEM((tiles, MP, FFN_TILE, width), x.dtype),
            pltpu.SemaphoreType.DMA((10,)),
            pltpu.SemaphoreType.DMA((2 * tiles,)),
        ],
        compiler_params=pltpu.CompilerParams(vmem_limit_bytes=VMEM),
        name="ffn",
    )(in_vmem(x), in_vmem(gain), *[in_hbm(w) for w in weights])


def squeeze_body(
    ids_ref,
    parts_ref,
    down_ref,
    other_ref,
    kept_out,
    given_out,
    squeezed_out,
    kept_ref,
    given_ref,
    squeezed_ref,
    sems,
):
    rows = parts_ref.shape[1]
    seqs = ids_ref.shape[0]
    seq = rows * CORES // seqs
    me = lax.axis_index("mp") % CORES
    for s in range(rows // seq):
        tile = slice(s * seq, (s + 1) * seq)
        task = ids_ref[me * (rows // seq) + s]
        ffout = []
        for core in range(CORES):
            total = parts_ref[core, tile].astype(jnp.float32)
            for i in range(1, CHIPS):
                total = total + parts_ref[CORES * i + core, tile].astype(jnp.float32)
            ffout.append(total)
        kept = jnp.where(me == 0, ffout[0], ffout[1]).astype(jnp.bfloat16)
        given = jnp.where(me == 0, ffout[1], ffout[0]).astype(jnp.bfloat16)
        kept_ref[tile] = kept
        given_ref[tile] = given
        sums = (matmul(kept, down_ref[task]) + matmul(given, other_ref[task])).astype(jnp.bfloat16)
        packed = slice(s // 2 * seq, (s // 2 + 1) * seq)
        squeezed_ref[packed, s % 2 * R : (s % 2 + 1) * R] = sums
    stores = [pltpu.make_async_copy(squeezed_ref, squeezed_out.at[i], sems.at[i]) for i in range(CHIPS)]
    stores.append(pltpu.make_async_copy(given_ref, given_out, sems.at[CHIPS]))
    stores.append(pltpu.make_async_copy(kept_ref, kept_out, sems.at[CHIPS + 1]))
    for store in stores:
        store.start()
    for store in stores:
        store.wait()


def squeeze(task_ids, parts, down, other):
    rows, width = parts.shape[1:]
    packed = (rows // 2, 2 * R)
    arrays = (parts, down, other)
    hbm = pl.BlockSpec(memory_space=pltpu.HBM)
    return pl.pallas_call(
        squeeze_body,
        out_shape=(
            pltpu.HBM((rows, width), parts.dtype),
            pltpu.HBM((rows, width), parts.dtype),
            pltpu.HBM((CHIPS, *packed), parts.dtype),
        ),
        in_specs=[pl.BlockSpec(memory_space=pltpu.SMEM)] + [whole(a) for a in arrays],
        out_specs=(hbm, hbm, hbm),
        scratch_shapes=[
            pltpu.VMEM((rows, width), parts.dtype),
            pltpu.VMEM((rows, width), parts.dtype),
            pltpu.VMEM(packed, parts.dtype),
            pltpu.SemaphoreType.DMA((CHIPS + 2,)),
        ],
        compiler_params=pltpu.CompilerParams(vmem_limit_bytes=VMEM),
        name="squeeze",
    )(task_ids, *[in_vmem(a) for a in arrays])


def relu_body(parts_ref, out_ref):
    total = parts_ref[0].astype(jnp.float32)
    for i in range(1, CHIPS):
        total = total + parts_ref[i].astype(jnp.float32)
    out_ref[...] = jnp.maximum(total, 0.0).astype(jnp.bfloat16)


def relu_sum(parts):
    out = jax.ShapeDtypeStruct(parts.shape[1:], parts.dtype)
    return call("relu_sum", relu_body, out, (parts,))


def expand_body(
    ids_ref, tokens_ref, mine_ref, theirs_ref, squeezed_ref, their_squeezed_ref, up_ref, out_ref
):
    seqs = ids_ref.shape[0]
    seq = tokens_ref.shape[0] // seqs
    per_core = seqs // CORES
    me = lax.axis_index("mp") % CORES
    for core in range(CORES):
        squeezed = jnp.where(me == core, squeezed_ref[...], their_squeezed_ref[...])
        for j in range(per_core):
            s = core * per_core + j
            tile = slice(s * seq, (s + 1) * seq)
            part = slice(j * seq, (j + 1) * seq)
            left = squeezed[j // 2 * seq : (j // 2 + 1) * seq, j % 2 * R : (j % 2 + 1) * R]
            expand = matmul_nt(left, up_ref[ids_ref[s]])
            ffout = jnp.where(me == core, mine_ref[part], theirs_ref[part])
            total = tokens_ref[tile].astype(jnp.float32) + ffout.astype(jnp.float32) + expand
            out_ref[tile] = total.astype(jnp.bfloat16)


def expand(task_ids, tokens, mine, theirs, squeezed, their_squeezed, up):
    out = jax.ShapeDtypeStruct(tokens.shape, tokens.dtype)
    arrays = (tokens, mine, theirs, squeezed, their_squeezed, up)
    return call("expand", expand_body, out, arrays, (task_ids,))


def hidden_body(layer_ref, task_table_ref, layer_table_ref, hyper_in_ref, out_ref):
    task_table = task_table_ref[...]
    row = layer_table_ref[pl.ds(layer_ref[0], 1)]
    embed = jnp.concatenate([task_table, jnp.broadcast_to(row, task_table.shape)], axis=1)
    hidden = jnp.maximum(matmul_nt(embed.astype(jnp.bfloat16), hyper_in_ref[...]), 0.0)
    for i in range(MP):
        out_ref[i] = hidden.astype(jnp.bfloat16)


def per_device(
    tokens,
    norm_gain,
    wi_gate,
    wi_linear,
    wo_out,
    task_table,
    layer_table,
    task_ids,
    layer_index,
    hyper_in,
    gen_down,
    gen_up,
):
    tok_dev, width = tokens.shape
    features = width * MP
    half = tok_dev // CORES
    core = lax.axis_index("mp") % CORES
    task_count = task_table.shape[0]

    halves = tokens.reshape(CORES, half, width)
    given = swap_cores(lax.dynamic_index_in_dim(halves, 1 - core, 0, keepdims=False))

    hidden = call(
        "hidden",
        hidden_body,
        jax.ShapeDtypeStruct((MP, task_count, hyper_in.shape[1]), jnp.bfloat16),
        (task_table, layer_table, hyper_in.T),
        (layer_index,),
        in_hbm,
    )

    hidden = exchange(hidden, "mp")
    hidden = jnp.moveaxis(hidden, 0, 1).reshape(task_count, -1)
    made_down, made_up = [
        matmul(hidden, generator).astype(jnp.bfloat16) for generator in (gen_down, gen_up)
    ]
    made = jnp.stack([made_down, swap_cores(made_down), made_up])
    made, sent, gate, linear, wo = lax.optimization_barrier(
        (made, spread(halves, given), wi_gate.T, wi_linear.T, wo_out)
    )
    gate_other, linear_other, wo_other = [swap_cores(w) for w in (gate, linear, wo)]
    gathered = exchange(sent, "mp", SAME_CORE)

    most = doubling_gather(made, "dp", (16, 1, 8, 4))
    downs = doubling_gather(most[:, :, :, :, :2], "dp", (2,))
    downs = jnp.transpose(downs, (5, 6, 4, 2, 1, 0, 3, 7))
    down, down_other = downs.reshape(2, task_count, width, R)
    ups = doubling_gather(most[:, :, :, :, 2], "dp", (2,))
    up = jnp.transpose(ups, (5, 4, 2, 1, 0, 3, 6)).reshape(task_count, width, R)

    partial = ffn(
        gathered,
        norm_gain.reshape(1, features),
        (gate, gate_other),
        (linear, linear_other),
        (wo, wo_other),
    )
    parts = exchange(partial, "mp", SAME_CORE)
    mine, given, squeeze_part = squeeze(task_ids, parts, down, down_other)
    theirs = swap_cores(given)
    squeezed = relu_sum(exchange(squeeze_part, "mp", SAME_CORE))
    return expand(task_ids, tokens, mine, theirs, squeezed, swap_cores(squeezed), up)


def solution(mesh):
    return jax.shard_map(
        per_device,
        mesh=mesh,
        in_specs=(
            P("dp", "mp"),
            P(),
            P(None, "mp"),
            P(None, "mp"),
            P("mp", None),
            P(),
            P(),
            P("dp"),
            P(),
            P(None, "mp"),
            P(None, ("mp", "dp")),
            P(None, ("mp", "dp")),
        ),
        out_specs=P("dp", "mp"),
        check_vma=False,
    )
```

```python
import jax
import jax.numpy as jnp
from jax import lax
from jax.experimental import pallas as pl
from jax.experimental.pallas import tpu as pltpu
from jax.sharding import PartitionSpec as P

R = 64
CORES = 2
CHIPS = 8
MP = CORES * CHIPS
SAME_CORE = [[chip * CORES + core for chip in range(CHIPS)] for core in range(CORES)]
VMEM = 32 * 1024 * 1024
FFN_TILE = 256


def matmul(left, right):
    return jnp.dot(left, right, preferred_element_type=jnp.float32)


def matmul_nt(left, right):
    return lax.dot_general(
        left, right, (((1,), (1,)), ((), ())), preferred_element_type=jnp.float32
    )


def exchange(pieces, axis, groups=None):
    return lax.all_to_all(
        pieces, axis, split_axis=0, concat_axis=0, axis_index_groups=groups, tiled=True
    )


def swap_cores(array):
    return lax.ppermute(array, "mp", [(i, i ^ 1) for i in range(MP)])


def doubling_gather(shard, axis, bits):
    index = lax.axis_index(axis)
    size = lax.axis_size(axis)
    held = shard
    for bit in bits:
        theirs = lax.ppermute(held, axis, [(i, i ^ bit) for i in range(size)])
        upper = (index & bit) != 0
        held = jnp.stack([jnp.where(upper, theirs, held), jnp.where(upper, held, theirs)])
    return held


def in_vmem(array):
    return pltpu.with_memory_space_constraint(array, pltpu.VMEM)


def in_hbm(array):
    return pltpu.with_memory_space_constraint(array, pltpu.HBM)


def whole(array):
    return pl.BlockSpec(memory_space=pltpu.VMEM)


def call(name, body, outs, arrays, scalars=(), place=in_vmem):
    return pl.pallas_call(
        body,
        out_shape=outs,
        in_specs=[pl.BlockSpec(memory_space=pltpu.SMEM) for _ in scalars] + [whole(a) for a in arrays],
        out_specs=jax.tree.map(lambda a: whole(a), outs),
        compiler_params=pltpu.CompilerParams(vmem_limit_bytes=VMEM),
        name=name,
    )(*scalars, *[place(a) for a in arrays])


def spread_body(tokens_ref, given_ref, out_ref, sems):
    me = lax.axis_index("mp") % CORES
    copies = []
    for i in range(CHIPS):
        first, second = out_ref.at[CORES * i + me], out_ref.at[CORES * i + 1 - me]
        copies.append(pltpu.make_async_copy(tokens_ref.at[me], first, sems.at[CORES * i]))
        copies.append(pltpu.make_async_copy(given_ref, second, sems.at[CORES * i + 1]))
    for copy in copies:
        copy.start()
    for copy in copies:
        copy.wait()


def spread(halves, given):
    return pl.pallas_call(
        spread_body,
        out_shape=pltpu.HBM((MP, *given.shape), given.dtype),
        in_specs=[whole(halves), whole(given)],
        out_specs=pl.BlockSpec(memory_space=pltpu.HBM),
        scratch_shapes=[pltpu.SemaphoreType.DMA((MP,))],
        name="spread",
    )(in_vmem(halves), in_vmem(given))


def ffn_body(
    x_ref,
    gain_ref,
    gate_ref,
    gate_other_ref,
    linear_ref,
    linear_other_ref,
    wo_own_ref,
    wo_other_ref,
    out_ref,
    normed_ref,
    wi_ref,
    wo_ref,
    sums_ref,
    in_sems,
    out_sems,
):
    rows, width = x_ref.shape[1:]
    hid, features = wo_ref.shape
    own = hid // 2
    sides = [slice(0, features // 2), slice(features // 2, features)]
    placed = [
        (source.at[:, side], wi_ref.at[pl.ds(i * own, own), side])
        for side in sides
        for i, source in enumerate((gate_ref, gate_other_ref, linear_ref, linear_other_ref))
    ]
    placed += [
        (wo_own_ref, wo_ref.at[pl.ds(0, own)]),
        (wo_other_ref, wo_ref.at[pl.ds(own, own)]),
    ]
    loads = [pltpu.make_async_copy(a, b, in_sems.at[i]) for i, (a, b) in enumerate(placed)]
    for load in loads:
        load.start()
    gain = gain_ref[...].astype(jnp.float32)
    tiles = [pl.ds(k * FFN_TILE, FFN_TILE) for k in range(rows // FFN_TILE)]
    for tile in tiles:
        wide = jnp.concatenate([x_ref[i, tile] for i in range(MP)], axis=1).astype(jnp.float32)
        scale = lax.rsqrt(jnp.mean(wide * wide, axis=-1, keepdims=True) + 1e-06)
        normed_ref[tile] = (wide * scale * gain).astype(jnp.bfloat16)
    stores = []
    for k, tile in enumerate(tiles):
        if k == 0:
            for load in loads[:4]:
                load.wait()
            both = matmul_nt(normed_ref[tile, sides[0]], wi_ref[:, sides[0]])
            for load in loads[4:8]:
                load.wait()
            both = both + matmul_nt(normed_ref[tile, sides[1]], wi_ref[:, sides[1]])
        else:
            both = matmul_nt(normed_ref[tile], wi_ref[...])
        act = (jax.nn.gelu(both[:, :hid], approximate=True) * both[:, hid:]).astype(jnp.bfloat16)
        if k == 0:
            for load in loads[8:]:
                load.wait()
        for j, side in enumerate(sides):
            sums = matmul(act, wo_ref[:, side]).astype(jnp.bfloat16)
            blocks = slice(j * MP // 2, (j + 1) * MP // 2)
            for i in range(MP // 2):
                sums_ref[k, j * MP // 2 + i] = sums[:, i * width : (i + 1) * width]
            store = pltpu.make_async_copy(
                sums_ref.at[k, blocks], out_ref.at[blocks, tile], out_sems.at[2 * k + j]
            )
            store.start()
            stores.append(store)
    for store in stores:
        store.wait()


def ffn(x, gain, gates, linears, wos):
    rows, width = x.shape[1:]
    own, features = wos[0].shape
    tiles = rows // FFN_TILE
    weights = (*gates, *linears, *wos)
    hbm = pl.BlockSpec(memory_space=pltpu.HBM)
    return pl.pallas_call(
        ffn_body,
        out_shape=pltpu.HBM(x.shape, x.dtype),
        in_specs=[whole(x), whole(gain)] + [hbm] * len(weights),
        out_specs=hbm,
        scratch_shapes=[
            pltpu.VMEM((rows, features), x.dtype),
            pltpu.VMEM((4 * own, features), x.dtype),
            pltpu.VMEM((2 * own, features), x.dtype),
            pltpu.VMEM((tiles, MP, FFN_TILE, width), x.dtype),
            pltpu.SemaphoreType.DMA((10,)),
            pltpu.SemaphoreType.DMA((2 * tiles,)),
        ],
        compiler_params=pltpu.CompilerParams(vmem_limit_bytes=VMEM),
        name="ffn",
    )(in_vmem(x), in_vmem(gain), *[in_hbm(w) for w in weights])


def squeeze_body(
    ids_ref,
    parts_ref,
    down_ref,
    other_ref,
    kept_out,
    given_out,
    squeezed_out,
    kept_ref,
    given_ref,
    squeezed_ref,
    sems,
):
    rows = parts_ref.shape[1]
    seqs = ids_ref.shape[0]
    seq = rows * CORES // seqs
    me = lax.axis_index("mp") % CORES
    for s in range(rows // seq):
        tile = slice(s * seq, (s + 1) * seq)
        task = ids_ref[me * (rows // seq) + s]
        ffout = []
        for core in range(CORES):
            total = parts_ref[core, tile].astype(jnp.float32)
            for i in range(1, CHIPS):
                total = total + parts_ref[CORES * i + core, tile].astype(jnp.float32)
            ffout.append(total)
        kept = jnp.where(me == 0, ffout[0], ffout[1]).astype(jnp.bfloat16)
        given = jnp.where(me == 0, ffout[1], ffout[0]).astype(jnp.bfloat16)
        kept_ref[tile] = kept
        given_ref[tile] = given
        sums = (matmul(kept, down_ref[task]) + matmul(given, other_ref[task])).astype(jnp.bfloat16)
        packed = slice(s // 2 * seq, (s // 2 + 1) * seq)
        squeezed_ref[packed, s % 2 * R : (s % 2 + 1) * R] = sums
    stores = [pltpu.make_async_copy(squeezed_ref, squeezed_out.at[i], sems.at[i]) for i in range(CHIPS)]
    stores.append(pltpu.make_async_copy(given_ref, given_out, sems.at[CHIPS]))
    stores.append(pltpu.make_async_copy(kept_ref, kept_out, sems.at[CHIPS + 1]))
    for store in stores:
        store.start()
    for store in stores:
        store.wait()


def squeeze(task_ids, parts, down, other):
    rows, width = parts.shape[1:]
    packed = (rows // 2, 2 * R)
    arrays = (parts, down, other)
    hbm = pl.BlockSpec(memory_space=pltpu.HBM)
    return pl.pallas_call(
        squeeze_body,
        out_shape=(
            pltpu.HBM((rows, width), parts.dtype),
            pltpu.HBM((rows, width), parts.dtype),
            pltpu.HBM((CHIPS, *packed), parts.dtype),
        ),
        in_specs=[pl.BlockSpec(memory_space=pltpu.SMEM)] + [whole(a) for a in arrays],
        out_specs=(hbm, hbm, hbm),
        scratch_shapes=[
            pltpu.VMEM((rows, width), parts.dtype),
            pltpu.VMEM((rows, width), parts.dtype),
            pltpu.VMEM(packed, parts.dtype),
            pltpu.SemaphoreType.DMA((CHIPS + 2,)),
        ],
        compiler_params=pltpu.CompilerParams(vmem_limit_bytes=VMEM),
        name="squeeze",
    )(task_ids, *[in_vmem(a) for a in arrays])


def relu_body(parts_ref, out_ref):
    total = parts_ref[0].astype(jnp.float32)
    for i in range(1, CHIPS):
        total = total + parts_ref[i].astype(jnp.float32)
    out_ref[...] = jnp.maximum(total, 0.0).astype(jnp.bfloat16)


def relu_sum(parts):
    out = jax.ShapeDtypeStruct(parts.shape[1:], parts.dtype)
    return call("relu_sum", relu_body, out, (parts,))


def expand_body(
    ids_ref, tokens_ref, mine_ref, theirs_ref, squeezed_ref, their_squeezed_ref, up_ref, out_ref
):
    seqs = ids_ref.shape[0]
    seq = tokens_ref.shape[0] // seqs
    per_core = seqs // CORES
    me = lax.axis_index("mp") % CORES
    for core in range(CORES):
        squeezed = jnp.where(me == core, squeezed_ref[...], their_squeezed_ref[...])
        for j in range(per_core):
            s = core * per_core + j
            tile = slice(s * seq, (s + 1) * seq)
            part = slice(j * seq, (j + 1) * seq)
            left = squeezed[j // 2 * seq : (j // 2 + 1) * seq, j % 2 * R : (j % 2 + 1) * R]
            expand = matmul_nt(left, up_ref[ids_ref[s]])
            ffout = jnp.where(me == core, mine_ref[part], theirs_ref[part])
            total = tokens_ref[tile].astype(jnp.float32) + ffout.astype(jnp.float32) + expand
            out_ref[tile] = total.astype(jnp.bfloat16)


def expand(task_ids, tokens, mine, theirs, squeezed, their_squeezed, up):
    out = jax.ShapeDtypeStruct(tokens.shape, tokens.dtype)
    arrays = (tokens, mine, theirs, squeezed, their_squeezed, up)
    return call("expand", expand_body, out, arrays, (task_ids,))


def hidden_body(layer_ref, task_table_ref, layer_table_ref, hyper_in_ref, out_ref):
    task_table = task_table_ref[...]
    row = layer_table_ref[pl.ds(layer_ref[0], 1)]
    embed = jnp.concatenate([task_table, jnp.broadcast_to(row, task_table.shape)], axis=1)
    hidden = jnp.maximum(matmul_nt(embed.astype(jnp.bfloat16), hyper_in_ref[...]), 0.0)
    tasks = hidden.shape[0] // 2
    packed = jnp.concatenate([hidden[:tasks], hidden[tasks:]], axis=1).astype(jnp.bfloat16)
    for i in range(MP):
        out_ref[i] = packed


def per_device(
    tokens,
    norm_gain,
    wi_gate,
    wi_linear,
    wo_out,
    task_table,
    layer_table,
    task_ids,
    layer_index,
    hyper_in,
    gen_down,
    gen_up,
):
    tok_dev, width = tokens.shape
    features = width * MP
    half = tok_dev // CORES
    core = lax.axis_index("mp") % CORES
    task_count = task_table.shape[0]

    halves = tokens.reshape(CORES, half, width)
    given = swap_cores(lax.dynamic_index_in_dim(halves, 1 - core, 0, keepdims=False))

    share = hyper_in.shape[1]
    hidden = call(
        "hidden",
        hidden_body,
        jax.ShapeDtypeStruct((MP, task_count // 2, 2 * share), jnp.bfloat16),
        (task_table, layer_table, hyper_in.T),
        (layer_index,),
        in_hbm,
    )

    hidden = exchange(hidden, "mp")
    hidden = jnp.concatenate([hidden[:, :, :share], hidden[:, :, share:]], axis=1)
    hidden = jnp.moveaxis(hidden, 0, 1).reshape(task_count, -1)
    made_down, made_up = [
        matmul(hidden, generator).astype(jnp.bfloat16) for generator in (gen_down, gen_up)
    ]
    made = jnp.stack([made_down, swap_cores(made_down), made_up])
    made, sent, gate, linear, wo = lax.optimization_barrier(
        (made, spread(halves, given), wi_gate.T, wi_linear.T, wo_out)
    )
    gate_other, linear_other, wo_other = [swap_cores(w) for w in (gate, linear, wo)]
    gathered = exchange(sent, "mp", SAME_CORE)

    most = doubling_gather(made, "dp", (16, 1, 8, 4))
    downs = doubling_gather(most[:, :, :, :, :2], "dp", (2,))
    downs = jnp.transpose(downs, (5, 6, 4, 2, 1, 0, 3, 7))
    down, down_other = downs.reshape(2, task_count, width, R)
    ups = doubling_gather(most[:, :, :, :, 2], "dp", (2,))
    up = jnp.transpose(ups, (5, 4, 2, 1, 0, 3, 6)).reshape(task_count, width, R)

    partial = ffn(
        gathered,
        norm_gain.reshape(1, features),
        (gate, gate_other),
        (linear, linear_other),
        (wo, wo_other),
    )
    parts = exchange(partial, "mp", SAME_CORE)
    mine, given, squeeze_part = squeeze(task_ids, parts, down, down_other)
    theirs = swap_cores(given)
    squeezed = relu_sum(exchange(squeeze_part, "mp", SAME_CORE))
    return expand(task_ids, tokens, mine, theirs, squeezed, swap_cores(squeezed), up)


def solution(mesh):
    return jax.shard_map(
        per_device,
        mesh=mesh,
        in_specs=(
            P("dp", "mp"),
            P(),
            P(None, "mp"),
            P(None, "mp"),
            P("mp", None),
            P(),
            P(),
            P("dp"),
            P(),
            P(None, "mp"),
            P(None, ("mp", "dp")),
            P(None, ("mp", "dp")),
        ),
        out_specs=P("dp", "mp"),
        check_vma=False,
    )
```

```python
import jax
import jax.numpy as jnp
from jax import lax
from jax.experimental import pallas as pl
from jax.experimental.pallas import tpu as pltpu
from jax.sharding import PartitionSpec as P

R = 64
CORES = 2
CHIPS = 8
MP = CORES * CHIPS
SAME_CORE = [[chip * CORES + core for chip in range(CHIPS)] for core in range(CORES)]
VMEM = 32 * 1024 * 1024
FFN_TILE = 256


def matmul(left, right):
    return jnp.dot(left, right, preferred_element_type=jnp.float32)


def matmul_nt(left, right):
    return lax.dot_general(
        left, right, (((1,), (1,)), ((), ())), preferred_element_type=jnp.float32
    )


def exchange(pieces, axis, groups=None):
    return lax.all_to_all(
        pieces, axis, split_axis=0, concat_axis=0, axis_index_groups=groups, tiled=True
    )


def swap_cores(array):
    return lax.ppermute(array, "mp", [(i, i ^ 1) for i in range(MP)])


def doubling_gather(shard, axis, bits):
    index = lax.axis_index(axis)
    size = lax.axis_size(axis)
    held = shard
    for bit in bits:
        theirs = lax.ppermute(held, axis, [(i, i ^ bit) for i in range(size)])
        upper = (index & bit) != 0
        held = jnp.stack([jnp.where(upper, theirs, held), jnp.where(upper, held, theirs)])
    return held


def in_vmem(array):
    return pltpu.with_memory_space_constraint(array, pltpu.VMEM)


def in_hbm(array):
    return pltpu.with_memory_space_constraint(array, pltpu.HBM)


def whole(array):
    return pl.BlockSpec(memory_space=pltpu.VMEM)


def call(name, body, outs, arrays, scalars=(), place=in_vmem):
    return pl.pallas_call(
        body,
        out_shape=outs,
        in_specs=[pl.BlockSpec(memory_space=pltpu.SMEM) for _ in scalars] + [whole(a) for a in arrays],
        out_specs=jax.tree.map(lambda a: whole(a), outs),
        compiler_params=pltpu.CompilerParams(vmem_limit_bytes=VMEM),
        name=name,
    )(*scalars, *[place(a) for a in arrays])


def spread_body(kept_ref, given_ref, out_ref, sems):
    me = lax.axis_index("mp") % CORES
    copies = []
    for i in range(CHIPS):
        first, second = out_ref.at[CORES * i + me], out_ref.at[CORES * i + 1 - me]
        copies.append(pltpu.make_async_copy(kept_ref, first, sems.at[CORES * i]))
        copies.append(pltpu.make_async_copy(given_ref, second, sems.at[CORES * i + 1]))
    for copy in copies:
        copy.start()
    for copy in copies:
        copy.wait()


def spread(kept, given):
    return pl.pallas_call(
        spread_body,
        out_shape=pltpu.HBM((MP, *given.shape), given.dtype),
        in_specs=[whole(kept), whole(given)],
        out_specs=pl.BlockSpec(memory_space=pltpu.HBM),
        scratch_shapes=[pltpu.SemaphoreType.DMA((MP,))],
        name="spread",
    )(in_vmem(kept), in_vmem(given))


def ffn_body(
    x_ref,
    gain_ref,
    gate_ref,
    gate_other_ref,
    linear_ref,
    linear_other_ref,
    wo_own_ref,
    wo_other_ref,
    out_ref,
    normed_ref,
    wi_ref,
    wo_ref,
    sums_ref,
    in_sems,
    out_sems,
):
    rows, width = x_ref.shape[1:]
    hid, features = wo_ref.shape
    own = hid // 2
    sides = [slice(0, features // 2), slice(features // 2, features)]
    placed = [
        (source.at[:, side], wi_ref.at[pl.ds(i * own, own), side])
        for side in sides
        for i, source in enumerate((gate_ref, gate_other_ref, linear_ref, linear_other_ref))
    ]
    placed += [
        (wo_own_ref, wo_ref.at[pl.ds(0, own)]),
        (wo_other_ref, wo_ref.at[pl.ds(own, own)]),
    ]
    loads = [pltpu.make_async_copy(a, b, in_sems.at[i]) for i, (a, b) in enumerate(placed)]
    for load in loads:
        load.start()
    gain = gain_ref[...].astype(jnp.float32)
    tiles = [pl.ds(k * FFN_TILE, FFN_TILE) for k in range(rows // FFN_TILE)]
    for tile in tiles:
        wide = jnp.concatenate([x_ref[i, tile] for i in range(MP)], axis=1).astype(jnp.float32)
        scale = lax.rsqrt(jnp.mean(wide * wide, axis=-1, keepdims=True) + 1e-06)
        normed_ref[tile] = (wide * scale * gain).astype(jnp.bfloat16)
    stores = []
    for k, tile in enumerate(tiles):
        if k == 0:
            for load in loads[:4]:
                load.wait()
            both = matmul_nt(normed_ref[tile, sides[0]], wi_ref[:, sides[0]])
            for load in loads[4:8]:
                load.wait()
            both = both + matmul_nt(normed_ref[tile, sides[1]], wi_ref[:, sides[1]])
        else:
            both = matmul_nt(normed_ref[tile], wi_ref[...])
        act = (jax.nn.gelu(both[:, :hid], approximate=True) * both[:, hid:]).astype(jnp.bfloat16)
        if k == 0:
            for load in loads[8:]:
                load.wait()
        for j, side in enumerate(sides):
            sums = matmul(act, wo_ref[:, side]).astype(jnp.bfloat16)
            blocks = slice(j * MP // 2, (j + 1) * MP // 2)
            for i in range(MP // 2):
                sums_ref[k, j * MP // 2 + i] = sums[:, i * width : (i + 1) * width]
            store = pltpu.make_async_copy(
                sums_ref.at[k, blocks], out_ref.at[blocks, tile], out_sems.at[2 * k + j]
            )
            store.start()
            stores.append(store)
    for store in stores:
        store.wait()


def ffn(x, gain, gates, linears, wos):
    rows, width = x.shape[1:]
    own, features = wos[0].shape
    tiles = rows // FFN_TILE
    weights = (*gates, *linears, *wos)
    hbm = pl.BlockSpec(memory_space=pltpu.HBM)
    return pl.pallas_call(
        ffn_body,
        out_shape=pltpu.HBM(x.shape, x.dtype),
        in_specs=[whole(x), whole(gain)] + [hbm] * len(weights),
        out_specs=hbm,
        scratch_shapes=[
            pltpu.VMEM((rows, features), x.dtype),
            pltpu.VMEM((4 * own, features), x.dtype),
            pltpu.VMEM((2 * own, features), x.dtype),
            pltpu.VMEM((tiles, MP, FFN_TILE, width), x.dtype),
            pltpu.SemaphoreType.DMA((10,)),
            pltpu.SemaphoreType.DMA((2 * tiles,)),
        ],
        compiler_params=pltpu.CompilerParams(vmem_limit_bytes=VMEM),
        name="ffn",
    )(in_vmem(x), in_vmem(gain), *[in_hbm(w) for w in weights])


def squeeze_body(
    ids_ref,
    parts_ref,
    down_ref,
    other_ref,
    kept_out,
    given_out,
    squeezed_out,
    kept_ref,
    given_ref,
    squeezed_ref,
    sems,
):
    rows = parts_ref.shape[1]
    seqs = ids_ref.shape[0]
    seq = rows * CORES // seqs
    me = lax.axis_index("mp") % CORES
    for s in range(rows // seq):
        tile = slice(s * seq, (s + 1) * seq)
        task = ids_ref[me * (rows // seq) + s]
        ffout = []
        for core in range(CORES):
            total = parts_ref[core, tile].astype(jnp.float32)
            for i in range(1, CHIPS):
                total = total + parts_ref[CORES * i + core, tile].astype(jnp.float32)
            ffout.append(total)
        kept = jnp.where(me == 0, ffout[0], ffout[1]).astype(jnp.bfloat16)
        given = jnp.where(me == 0, ffout[1], ffout[0]).astype(jnp.bfloat16)
        kept_ref[tile] = kept
        given_ref[tile] = given
        sums = (matmul(kept, down_ref[task]) + matmul(given, other_ref[task])).astype(jnp.bfloat16)
        packed = slice(s // 2 * seq, (s // 2 + 1) * seq)
        squeezed_ref[packed, s % 2 * R : (s % 2 + 1) * R] = sums
    stores = [pltpu.make_async_copy(squeezed_ref, squeezed_out.at[i], sems.at[i]) for i in range(CHIPS)]
    stores.append(pltpu.make_async_copy(given_ref, given_out, sems.at[CHIPS]))
    stores.append(pltpu.make_async_copy(kept_ref, kept_out, sems.at[CHIPS + 1]))
    for store in stores:
        store.start()
    for store in stores:
        store.wait()


def squeeze(task_ids, parts, down, other):
    rows, width = parts.shape[1:]
    packed = (rows // 2, 2 * R)
    arrays = (parts, down, other)
    hbm = pl.BlockSpec(memory_space=pltpu.HBM)
    return pl.pallas_call(
        squeeze_body,
        out_shape=(
            pltpu.HBM((rows, width), parts.dtype),
            pltpu.HBM((rows, width), parts.dtype),
            pltpu.HBM((CHIPS, *packed), parts.dtype),
        ),
        in_specs=[pl.BlockSpec(memory_space=pltpu.SMEM)] + [whole(a) for a in arrays],
        out_specs=(hbm, hbm, hbm),
        scratch_shapes=[
            pltpu.VMEM((rows, width), parts.dtype),
            pltpu.VMEM((rows, width), parts.dtype),
            pltpu.VMEM(packed, parts.dtype),
            pltpu.SemaphoreType.DMA((CHIPS + 2,)),
        ],
        compiler_params=pltpu.CompilerParams(vmem_limit_bytes=VMEM),
        name="squeeze",
    )(task_ids, *[in_vmem(a) for a in arrays])


def relu_body(parts_ref, out_ref):
    total = parts_ref[0].astype(jnp.float32)
    for i in range(1, CHIPS):
        total = total + parts_ref[i].astype(jnp.float32)
    out_ref[...] = jnp.maximum(total, 0.0).astype(jnp.bfloat16)


def relu_sum(parts):
    out = jax.ShapeDtypeStruct(parts.shape[1:], parts.dtype)
    return call("relu_sum", relu_body, out, (parts,))


def expand_body(
    ids_ref, tokens_ref, mine_ref, theirs_ref, squeezed_ref, their_squeezed_ref, up_ref, out_ref
):
    seqs = ids_ref.shape[0]
    seq = tokens_ref.shape[0] // seqs
    per_core = seqs // CORES
    me = lax.axis_index("mp") % CORES
    for core in range(CORES):
        squeezed = jnp.where(me == core, squeezed_ref[...], their_squeezed_ref[...])
        for j in range(per_core):
            s = core * per_core + j
            tile = slice(s * seq, (s + 1) * seq)
            part = slice(j * seq, (j + 1) * seq)
            left = squeezed[j // 2 * seq : (j // 2 + 1) * seq, j % 2 * R : (j % 2 + 1) * R]
            expand = matmul_nt(left, up_ref[ids_ref[s]])
            ffout = jnp.where(me == core, mine_ref[part], theirs_ref[part])
            total = tokens_ref[tile].astype(jnp.float32) + ffout.astype(jnp.float32) + expand
            out_ref[tile] = total.astype(jnp.bfloat16)


def expand(task_ids, tokens, mine, theirs, squeezed, their_squeezed, up):
    out = jax.ShapeDtypeStruct(tokens.shape, tokens.dtype)
    arrays = (tokens, mine, theirs, squeezed, their_squeezed, up)
    return call("expand", expand_body, out, arrays, (task_ids,))


def hidden_body(layer_ref, task_table_ref, layer_table_ref, hyper_in_ref, out_ref):
    task_table = task_table_ref[...]
    row = layer_table_ref[pl.ds(layer_ref[0], 1)]
    embed = jnp.concatenate([task_table, jnp.broadcast_to(row, task_table.shape)], axis=1)
    hidden = jnp.maximum(matmul_nt(embed.astype(jnp.bfloat16), hyper_in_ref[...]), 0.0)
    for i in range(MP):
        out_ref[i] = hidden.astype(jnp.bfloat16)


def per_device(
    tokens,
    norm_gain,
    wi_gate,
    wi_linear,
    wo_out,
    task_table,
    layer_table,
    task_ids,
    layer_index,
    hyper_in,
    gen_down,
    gen_up,
):
    tok_dev, width = tokens.shape
    features = width * MP
    half = tok_dev // CORES
    core = lax.axis_index("mp") % CORES
    task_count = task_table.shape[0]

    halves = tokens.reshape(CORES, half, width)
    kept = lax.dynamic_index_in_dim(halves, core, 0, keepdims=False)
    given = swap_cores(lax.dynamic_index_in_dim(halves, 1 - core, 0, keepdims=False))

    hidden = call(
        "hidden",
        hidden_body,
        jax.ShapeDtypeStruct((MP, task_count, hyper_in.shape[1]), jnp.bfloat16),
        (task_table, layer_table, hyper_in.T),
        (layer_index,),
        in_hbm,
    )

    hidden = exchange(hidden, "mp")
    hidden = jnp.moveaxis(hidden, 0, 1).reshape(task_count, -1)
    made_down, made_up = [
        matmul(hidden, generator).astype(jnp.bfloat16) for generator in (gen_down, gen_up)
    ]
    made = jnp.stack([made_down, swap_cores(made_down), made_up])
    made, sent, gate, linear, wo = lax.optimization_barrier(
        (made, spread(kept, given), wi_gate.T, wi_linear.T, wo_out)
    )
    gate_other, linear_other, wo_other = [swap_cores(w) for w in (gate, linear, wo)]
    gathered = exchange(sent, "mp", SAME_CORE)

    most = doubling_gather(made, "dp", (16, 1, 8, 4))
    downs = doubling_gather(most[:, :, :, :, :2], "dp", (2,))
    downs = jnp.transpose(downs, (5, 6, 4, 2, 1, 0, 3, 7))
    down, down_other = downs.reshape(2, task_count, width, R)
    ups = doubling_gather(most[:, :, :, :, 2], "dp", (2,))
    up = jnp.transpose(ups, (5, 4, 2, 1, 0, 3, 6)).reshape(task_count, width, R)

    partial = ffn(
        gathered,
        norm_gain.reshape(1, features),
        (gate, gate_other),
        (linear, linear_other),
        (wo, wo_other),
    )
    parts = exchange(partial, "mp", SAME_CORE)
    mine, given, squeeze_part = squeeze(task_ids, parts, down, down_other)
    theirs = swap_cores(given)
    squeezed = relu_sum(exchange(squeeze_part, "mp", SAME_CORE))
    return expand(task_ids, tokens, mine, theirs, squeezed, swap_cores(squeezed), up)


def solution(mesh):
    return jax.shard_map(
        per_device,
        mesh=mesh,
        in_specs=(
            P("dp", "mp"),
            P(),
            P(None, "mp"),
            P(None, "mp"),
            P("mp", None),
            P(),
            P(),
            P("dp"),
            P(),
            P(None, "mp"),
            P(None, ("mp", "dp")),
            P(None, ("mp", "dp")),
        ),
        out_specs=P("dp", "mp"),
        check_vma=False,
    )
```

```python
import jax
import jax.numpy as jnp
from jax import lax
from jax.experimental import pallas as pl
from jax.experimental.pallas import tpu as pltpu
from jax.sharding import PartitionSpec as P

R = 64
CORES = 2
CHIPS = 8
MP = CORES * CHIPS
SAME_CORE = [[chip * CORES + core for chip in range(CHIPS)] for core in range(CORES)]
VMEM = 32 * 1024 * 1024
FFN_TILE = 256


def matmul(left, right):
    return jnp.dot(left, right, preferred_element_type=jnp.float32)


def matmul_nt(left, right):
    return lax.dot_general(
        left, right, (((1,), (1,)), ((), ())), preferred_element_type=jnp.float32
    )


def exchange(pieces, axis, groups=None):
    return lax.all_to_all(
        pieces, axis, split_axis=0, concat_axis=0, axis_index_groups=groups, tiled=True
    )


def swap_cores(array):
    return lax.ppermute(array, "mp", [(i, i ^ 1) for i in range(MP)])


def doubling_gather(shard, axis, bits):
    index = lax.axis_index(axis)
    size = lax.axis_size(axis)
    held = shard
    for bit in bits:
        theirs = lax.ppermute(held, axis, [(i, i ^ bit) for i in range(size)])
        upper = (index & bit) != 0
        held = jnp.stack([jnp.where(upper, theirs, held), jnp.where(upper, held, theirs)])
    return held


def in_vmem(array):
    return pltpu.with_memory_space_constraint(array, pltpu.VMEM)


def in_hbm(array):
    return pltpu.with_memory_space_constraint(array, pltpu.HBM)


def whole(array):
    return pl.BlockSpec(memory_space=pltpu.VMEM)


def call(name, body, outs, arrays, scalars=(), place=in_vmem):
    return pl.pallas_call(
        body,
        out_shape=outs,
        in_specs=[pl.BlockSpec(memory_space=pltpu.SMEM) for _ in scalars] + [whole(a) for a in arrays],
        out_specs=jax.tree.map(lambda a: whole(a), outs),
        compiler_params=pltpu.CompilerParams(vmem_limit_bytes=VMEM),
        name=name,
    )(*scalars, *[place(a) for a in arrays])


def spread_body(kept_ref, given_ref, out_ref, sems):
    me = lax.axis_index("mp") % CORES
    copies = []
    for i in range(CHIPS):
        first, second = out_ref.at[CORES * i + me], out_ref.at[CORES * i + 1 - me]
        copies.append(pltpu.make_async_copy(kept_ref, first, sems.at[CORES * i]))
        copies.append(pltpu.make_async_copy(given_ref, second, sems.at[CORES * i + 1]))
    for copy in copies:
        copy.start()
    for copy in copies:
        copy.wait()


def spread(kept, given):
    return pl.pallas_call(
        spread_body,
        out_shape=pltpu.HBM((MP, *given.shape), given.dtype),
        in_specs=[whole(kept), whole(given)],
        out_specs=pl.BlockSpec(memory_space=pltpu.HBM),
        scratch_shapes=[pltpu.SemaphoreType.DMA((MP,))],
        name="spread",
    )(in_vmem(kept), in_vmem(given))


def ffn_body(
    x_ref,
    gain_ref,
    gate_ref,
    gate_other_ref,
    linear_ref,
    linear_other_ref,
    wo_own_ref,
    wo_other_ref,
    out_ref,
    normed_ref,
    wi_ref,
    wo_ref,
    sums_ref,
    in_sems,
    out_sems,
):
    rows, width = x_ref.shape[1:]
    hid, features = wo_ref.shape
    own = hid // 2
    sides = [slice(0, features // 2), slice(features // 2, features)]
    placed = [
        (source.at[:, side], wi_ref.at[pl.ds(i * own, own), side])
        for side in sides
        for i, source in enumerate((gate_ref, gate_other_ref, linear_ref, linear_other_ref))
    ]
    placed += [
        (wo_own_ref, wo_ref.at[pl.ds(0, own)]),
        (wo_other_ref, wo_ref.at[pl.ds(own, own)]),
    ]
    loads = [pltpu.make_async_copy(a, b, in_sems.at[i]) for i, (a, b) in enumerate(placed)]
    for load in loads:
        load.start()
    gain = gain_ref[...].astype(jnp.float32)
    tiles = [pl.ds(k * FFN_TILE, FFN_TILE) for k in range(rows // FFN_TILE)]
    for tile in tiles:
        wide = jnp.concatenate([x_ref[i, tile] for i in range(MP)], axis=1).astype(jnp.float32)
        scale = lax.rsqrt(jnp.mean(wide * wide, axis=-1, keepdims=True) + 1e-06)
        normed_ref[tile] = (wide * scale * gain).astype(jnp.bfloat16)
    stores = []
    for k, tile in enumerate(tiles):
        if k == 0:
            for load in loads[:4]:
                load.wait()
            both = matmul_nt(normed_ref[tile, sides[0]], wi_ref[:, sides[0]])
            for load in loads[4:8]:
                load.wait()
            both = both + matmul_nt(normed_ref[tile, sides[1]], wi_ref[:, sides[1]])
        else:
            both = matmul_nt(normed_ref[tile], wi_ref[...])
        act = (jax.nn.gelu(both[:, :hid], approximate=True) * both[:, hid:]).astype(jnp.bfloat16)
        if k == 0:
            for load in loads[8:]:
                load.wait()
        for j, side in enumerate(sides):
            sums = matmul(act, wo_ref[:, side]).astype(jnp.bfloat16)
            blocks = slice(j * MP // 2, (j + 1) * MP // 2)
            for i in range(MP // 2):
                sums_ref[k, j * MP // 2 + i] = sums[:, i * width : (i + 1) * width]
            store = pltpu.make_async_copy(
                sums_ref.at[k, blocks], out_ref.at[blocks, tile], out_sems.at[2 * k + j]
            )
            store.start()
            stores.append(store)
    for store in stores:
        store.wait()


def ffn(x, gain, gates, linears, wos):
    rows, width = x.shape[1:]
    own, features = wos[0].shape
    tiles = rows // FFN_TILE
    weights = (*gates, *linears, *wos)
    hbm = pl.BlockSpec(memory_space=pltpu.HBM)
    return pl.pallas_call(
        ffn_body,
        out_shape=pltpu.HBM(x.shape, x.dtype),
        in_specs=[whole(x), whole(gain)] + [hbm] * len(weights),
        out_specs=hbm,
        scratch_shapes=[
            pltpu.VMEM((rows, features), x.dtype),
            pltpu.VMEM((4 * own, features), x.dtype),
            pltpu.VMEM((2 * own, features), x.dtype),
            pltpu.VMEM((tiles, MP, FFN_TILE, width), x.dtype),
            pltpu.SemaphoreType.DMA((10,)),
            pltpu.SemaphoreType.DMA((2 * tiles,)),
        ],
        compiler_params=pltpu.CompilerParams(vmem_limit_bytes=VMEM),
        name="ffn",
    )(in_vmem(x), in_vmem(gain), *[in_hbm(w) for w in weights])


def squeeze_body(
    ids_ref,
    parts_ref,
    down_ref,
    other_ref,
    kept_out,
    given_out,
    squeezed_out,
    kept_ref,
    given_ref,
    squeezed_ref,
    sems,
):
    rows = parts_ref.shape[1]
    seqs = ids_ref.shape[0]
    seq = rows * CORES // seqs
    me = lax.axis_index("mp") % CORES
    early = []
    for s in range(rows // seq):
        tile = slice(s * seq, (s + 1) * seq)
        task = ids_ref[me * (rows // seq) + s]
        ffout = []
        for core in range(CORES):
            total = parts_ref[core, tile].astype(jnp.float32)
            for i in range(1, CHIPS):
                total = total + parts_ref[CORES * i + core, tile].astype(jnp.float32)
            ffout.append(total)
        kept = jnp.where(me == 0, ffout[0], ffout[1]).astype(jnp.bfloat16)
        given = jnp.where(me == 0, ffout[1], ffout[0]).astype(jnp.bfloat16)
        kept_ref[tile] = kept
        given_ref[tile] = given
        here = pl.ds(s * seq, seq)
        for i, pair in enumerate(((given_ref, given_out), (kept_ref, kept_out))):
            sem = sems.at[CHIPS + 2 * s + i]
            early.append(pltpu.make_async_copy(pair[0].at[here], pair[1].at[here], sem))
            early[-1].start()
        sums = (matmul(kept, down_ref[task]) + matmul(given, other_ref[task])).astype(jnp.bfloat16)
        packed = slice(s // 2 * seq, (s // 2 + 1) * seq)
        squeezed_ref[packed, s % 2 * R : (s % 2 + 1) * R] = sums
    stores = [pltpu.make_async_copy(squeezed_ref, squeezed_out.at[i], sems.at[i]) for i in range(CHIPS)]
    for store in stores:
        store.start()
    for store in early + stores:
        store.wait()


def squeeze(task_ids, parts, down, other):
    rows, width = parts.shape[1:]
    packed = (rows // 2, 2 * R)
    arrays = (parts, down, other)
    hbm = pl.BlockSpec(memory_space=pltpu.HBM)
    return pl.pallas_call(
        squeeze_body,
        out_shape=(
            pltpu.HBM((rows, width), parts.dtype),
            pltpu.HBM((rows, width), parts.dtype),
            pltpu.HBM((CHIPS, *packed), parts.dtype),
        ),
        in_specs=[pl.BlockSpec(memory_space=pltpu.SMEM)] + [whole(a) for a in arrays],
        out_specs=(hbm, hbm, hbm),
        scratch_shapes=[
            pltpu.VMEM((rows, width), parts.dtype),
            pltpu.VMEM((rows, width), parts.dtype),
            pltpu.VMEM(packed, parts.dtype),
            pltpu.SemaphoreType.DMA((2 * CHIPS,)),
        ],
        compiler_params=pltpu.CompilerParams(vmem_limit_bytes=VMEM),
        name="squeeze",
    )(task_ids, *[in_vmem(a) for a in arrays])


def relu_body(parts_ref, out_ref):
    total = parts_ref[0].astype(jnp.float32)
    for i in range(1, CHIPS):
        total = total + parts_ref[i].astype(jnp.float32)
    out_ref[...] = jnp.maximum(total, 0.0).astype(jnp.bfloat16)


def relu_sum(parts):
    out = jax.ShapeDtypeStruct(parts.shape[1:], parts.dtype)
    return call("relu_sum", relu_body, out, (parts,))


def expand_body(
    ids_ref, tokens_ref, mine_ref, theirs_ref, squeezed_ref, their_squeezed_ref, up_ref, out_ref
):
    seqs = ids_ref.shape[0]
    seq = tokens_ref.shape[0] // seqs
    per_core = seqs // CORES
    me = lax.axis_index("mp") % CORES
    for core in range(CORES):
        squeezed = jnp.where(me == core, squeezed_ref[...], their_squeezed_ref[...])
        for j in range(per_core):
            s = core * per_core + j
            tile = slice(s * seq, (s + 1) * seq)
            part = slice(j * seq, (j + 1) * seq)
            left = squeezed[j // 2 * seq : (j // 2 + 1) * seq, j % 2 * R : (j % 2 + 1) * R]
            expand = matmul_nt(left, up_ref[ids_ref[s]])
            ffout = jnp.where(me == core, mine_ref[part], theirs_ref[part])
            total = tokens_ref[tile].astype(jnp.float32) + ffout.astype(jnp.float32) + expand
            out_ref[tile] = total.astype(jnp.bfloat16)


def expand(task_ids, tokens, mine, theirs, squeezed, their_squeezed, up):
    out = jax.ShapeDtypeStruct(tokens.shape, tokens.dtype)
    arrays = (tokens, mine, theirs, squeezed, their_squeezed, up)
    return call("expand", expand_body, out, arrays, (task_ids,))


def hidden_body(layer_ref, task_table_ref, layer_table_ref, hyper_in_ref, out_ref):
    task_table = task_table_ref[...]
    row = layer_table_ref[pl.ds(layer_ref[0], 1)]
    embed = jnp.concatenate([task_table, jnp.broadcast_to(row, task_table.shape)], axis=1)
    hidden = jnp.maximum(matmul_nt(embed.astype(jnp.bfloat16), hyper_in_ref[...]), 0.0)
    for i in range(MP):
        out_ref[i] = hidden.astype(jnp.bfloat16)


def per_device(
    tokens,
    norm_gain,
    wi_gate,
    wi_linear,
    wo_out,
    task_table,
    layer_table,
    task_ids,
    layer_index,
    hyper_in,
    gen_down,
    gen_up,
):
    tok_dev, width = tokens.shape
    features = width * MP
    half = tok_dev // CORES
    core = lax.axis_index("mp") % CORES
    task_count = task_table.shape[0]

    halves = tokens.reshape(CORES, half, width)
    kept = lax.dynamic_index_in_dim(halves, core, 0, keepdims=False)
    given = swap_cores(lax.dynamic_index_in_dim(halves, 1 - core, 0, keepdims=False))

    hidden = call(
        "hidden",
        hidden_body,
        jax.ShapeDtypeStruct((MP, task_count, hyper_in.shape[1]), jnp.bfloat16),
        (task_table, layer_table, hyper_in.T),
        (layer_index,),
        in_hbm,
    )

    hidden = exchange(hidden, "mp")
    hidden = jnp.moveaxis(hidden, 0, 1).reshape(task_count, -1)
    made_down, made_up = [
        matmul(hidden, generator).astype(jnp.bfloat16) for generator in (gen_down, gen_up)
    ]
    made = jnp.stack([made_down, swap_cores(made_down), made_up])
    made, sent, gate, linear, wo = lax.optimization_barrier(
        (made, spread(kept, given), wi_gate.T, wi_linear.T, wo_out)
    )
    gate_other, linear_other, wo_other = [swap_cores(w) for w in (gate, linear, wo)]
    gathered = exchange(sent, "mp", SAME_CORE)

    most = doubling_gather(made, "dp", (16, 1, 8, 4))
    downs = doubling_gather(most[:, :, :, :, :2], "dp", (2,))
    downs = jnp.transpose(downs, (5, 6, 4, 2, 1, 0, 3, 7))
    down, down_other = downs.reshape(2, task_count, width, R)
    ups = doubling_gather(most[:, :, :, :, 2], "dp", (2,))
    up = jnp.transpose(ups, (5, 4, 2, 1, 0, 3, 6)).reshape(task_count, width, R)

    partial = ffn(
        gathered,
        norm_gain.reshape(1, features),
        (gate, gate_other),
        (linear, linear_other),
        (wo, wo_other),
    )
    parts = exchange(partial, "mp", SAME_CORE)
    mine, given, squeeze_part = squeeze(task_ids, parts, down, down_other)
    theirs = swap_cores(given)
    squeezed = relu_sum(exchange(squeeze_part, "mp", SAME_CORE))
    return expand(task_ids, tokens, mine, theirs, squeezed, swap_cores(squeezed), up)


def solution(mesh):
    return jax.shard_map(
        per_device,
        mesh=mesh,
        in_specs=(
            P("dp", "mp"),
            P(),
            P(None, "mp"),
            P(None, "mp"),
            P("mp", None),
            P(),
            P(),
            P("dp"),
            P(),
            P(None, "mp"),
            P(None, ("mp", "dp")),
            P(None, ("mp", "dp")),
        ),
        out_specs=P("dp", "mp"),
        check_vma=False,
    )
```
